256 devices in a mesh: rep: 8 (over y, x_hi), blk: 32 (over z, x_lo, core).
Axes of the slice: x: 4 (x_hi: 2, x_lo: 2; x = x_hi * 2 + x_lo), y: 4, z: 8, core: 2. Of those that a mesh axis runs over, the one named last changes fastest.
Arguments:
- node_features: bfloat16 [65536, 256], P(('rep', 'blk')), may hold values from -6 to 6
- tile_values: bfloat16 [8, 32, 128, 128, 128], P('rep', 'blk'), may hold values from -0.09375 to 0.09375
- tile_row: int32 [8, 32, 128], P('rep', 'blk'), may hold values from 0 to 15, as said below
- tile_col: int32 [8, 32, 128], P('rep', 'blk'), may hold values from 0 to 63
- tile_count: int32 [8, 32], P('rep', 'blk'), may hold values from 16 to 128, as said below
- weight: bfloat16 [256, 256], replicated, may hold values from -0.375 to 0.375
- cotangent: bfloat16 [32, 8, 256, 256], P('blk', 'rep'), may hold values from -6 to 6
Outputs:
- layer_out: bfloat16 [32, 8, 256, 256], P('blk', 'rep')
- grad_weight: float32 [256, 256], replicated
- grad_features: bfloat16 [65536, 256], P(('rep', 'blk'))
The draws below stay inside these ranges and needn't reach their ends.
Inputs may be any that keep to these rules, and one draw needn't show every extreme that they name: `tile_row`: within one device the live slots name distinct tile pairs. Slots 0 to tile_count - 1 of a device are live, the rest are ignored; some device has all 128 slots live.
All inputs are finite; a program needn't handle non-finite values.
Results may differ from the reference program's by a relative error of at most 0.03.
Values may be sent and summed in bfloat16 or wider, within the bound.
No kernel may reach another device: no remote copies, remote signals or barrier semaphores. Data moves between devices by JAX's collectives and lax.ppermute only.
A program may use at most 128 MiB of HBM per device.

```python
import jax
import jax.numpy as jnp
from jax import lax

F = 256
TILE = 128
XR = 256
SLAB = 2048
GROUP = 8192
SLAB_BLOCKS = 16
GROUP_BLOCKS = 64
TILES_DEV = 128
NODES = 65536
N_REP = 8
N_BLK = 32


def tile_pairs(key):
    pair_key = jax.random.fold_in(key, 7)

    def one_device(device_index):
        return jax.random.permutation(jax.random.fold_in(pair_key, device_index), SLAB_BLOCKS * GROUP_BLOCKS)[:TILES_DEV]
    chosen = jax.vmap(one_device)(jnp.arange(N_REP * N_BLK, dtype=jnp.int32))
    return chosen.reshape(N_REP, N_BLK, TILES_DEV).astype(jnp.int32)


def draw_tile_row(key, part):
    return (tile_pairs(key) // GROUP_BLOCKS).astype(jnp.int32)


def draw_tile_col(key, part):
    return (tile_pairs(key) % GROUP_BLOCKS).astype(jnp.int32)


def draw_tile_count(key, part):
    halvings = jax.random.randint(jax.random.fold_in(key, 11), (N_REP * N_BLK,), 0, 4)
    counts = jnp.maximum(TILES_DEV // 2 ** halvings, 1)
    fullest = jax.random.randint(jax.random.fold_in(key, 13), (), 0, N_REP * N_BLK)
    counts = jnp.where(jnp.arange(N_REP * N_BLK, dtype=jnp.int32) == fullest, TILES_DEV, counts)
    return counts.reshape(N_REP, N_BLK).astype(jnp.int32)


def block_scale(key, shape, shards, smallest, largest):
    def one(dim, shards_of):
        heights = jax.random.uniform(jax.random.fold_in(jax.random.fold_in(key, 6), dim), (shards_of,), jnp.float32, smallest / len(shards), largest / len(shards))
        return jnp.repeat(jnp.exp(heights), shape[dim] // shards_of).reshape((-1,) + (1,) * (len(shape) - dim - 1))

    gain = one(*shards[0])
    for cut in shards[1:]:
        gain = gain * one(*cut)
    return gain


def centred(rng, extent, scale, reach, split=(), kind=jnp.bfloat16):
    gain = block_scale(rng, extent, split, -0.22, 0.18) if split else 1.0
    values = jax.random.normal(rng, extent, jnp.float32) * scale * gain
    return jnp.minimum(jnp.maximum(values, -reach), reach).astype(kind)


def setup_inputs(seed: int = 0) -> dict:
    arg_keys = jax.random.split(jax.random.key(seed), 8)
    return {
        "node_features": centred(arg_keys[0], (NODES, F), 1.0, 6.0, ((0, 256),)),
        "tile_values": centred(arg_keys[1], (N_REP, N_BLK, TILES_DEV, TILE, TILE), (TILE * TILES_DEV * N_REP // (2 * SLAB_BLOCKS)) ** -0.5, 0.09375, ((0, 8), (1, 32))),
        "tile_row": draw_tile_row(jax.random.fold_in(arg_keys[7], 71), 0),
        "tile_col": draw_tile_col(jax.random.fold_in(arg_keys[7], 71), 0),
        "tile_count": draw_tile_count(jax.random.fold_in(arg_keys[7], 71), 0),
        "weight": centred(arg_keys[5], (F, F), F ** -0.5, 0.375),
        "cotangent": centred(arg_keys[6], (N_BLK, N_REP, XR, F), 1.0, 6.0, ((0, 32), (1, 8))),
    }


def reference(node_features, tile_values, tile_row, tile_col, tile_count, weight, cotangent):
    groups = node_features.reshape(N_REP, GROUP_BLOCKS, TILE, F)
    live_mask = (jnp.arange(TILES_DEV, dtype=jnp.int32)[None, None, :] < tile_count[:, :, None]).astype(jnp.float32)
    row_hot = (tile_row[..., None] == jnp.arange(SLAB_BLOCKS, dtype=jnp.int32)).astype(jnp.float32) * live_mask[..., None]
    col_hot = (tile_col[..., None] == jnp.arange(GROUP_BLOCKS, dtype=jnp.int32)).astype(jnp.float32) * live_mask[..., None]

    def forward_slab(slab_index):
        def one_group(group_index):
            picked = jnp.take(groups[group_index], tile_col[group_index, slab_index], axis=0)
            products = jnp.einsum('tij,tjf->tif', tile_values[group_index, slab_index].astype(jnp.float32), picked.astype(jnp.float32))
            partial_value = jnp.einsum('tk,tif->kif', row_hot[group_index, slab_index], products)
            return lax.optimization_barrier(partial_value.astype(jnp.bfloat16)).astype(jnp.float32)

        partials = lax.map(one_group, jnp.arange(N_REP, dtype=jnp.int32))
        return jnp.sum(partials, axis=0).reshape(SLAB, F).astype(jnp.bfloat16)

    hidden = lax.map(forward_slab, jnp.arange(N_BLK, dtype=jnp.int32))
    hidden_rows = hidden.reshape(NODES, F)
    preact = jnp.dot(hidden_rows, weight, preferred_element_type=jnp.float32)
    gating = jax.nn.sigmoid(preact)
    layer_out = (preact * gating).astype(jnp.bfloat16).reshape(N_BLK, N_REP, XR, F)
    slope_term = gating * (1.0 + preact * (1.0 - gating))
    grad_pre = (cotangent.reshape(NODES, F).astype(jnp.float32) * slope_term).astype(jnp.bfloat16)
    grad_weight = jnp.dot(hidden_rows.T, grad_pre, preferred_element_type=jnp.float32)
    grad_hidden = jnp.dot(grad_pre, weight.T, preferred_element_type=jnp.float32).astype(jnp.bfloat16)
    grad_blocks = grad_hidden.reshape(N_BLK, SLAB_BLOCKS, TILE, F)

    def backward_group(group_index):
        def add_slab(total, slab_index):
            picked = jnp.take(grad_blocks[slab_index], tile_row[group_index, slab_index], axis=0)
            products = jnp.einsum('tij,tif->tjf', tile_values[group_index, slab_index].astype(jnp.float32), picked.astype(jnp.float32))
            partial_value = jnp.einsum('tk,tjf->kjf', col_hot[group_index, slab_index], products)
            partial_value = lax.optimization_barrier(partial_value.astype(jnp.bfloat16)).astype(jnp.float32)
            return total + partial_value, None

        total, unused = lax.scan(add_slab, jnp.zeros((GROUP_BLOCKS, TILE, F), jnp.float32), jnp.arange(N_BLK, dtype=jnp.int32))
        return total.reshape(GROUP, F).astype(jnp.bfloat16)

    grad_features = lax.map(backward_group, jnp.arange(N_REP, dtype=jnp.int32)).reshape(NODES, F)
    return (layer_out, grad_weight, grad_features)
```

```python
import jax
import jax.numpy as jnp
import numpy as np
from jax import lax
from jax.experimental import pallas as pl
from jax.experimental.pallas import tpu as pltpu
from jax.sharding import Mesh
from jax.sharding import PartitionSpec as P

REP = ("y", "xh")
BLK = ("z", "xl", "core")
N_Z = 8
TILE = 128
F = 256
XR = 256
N_REP = 8
SLOTS = 128
ROW_BLOCKS = 16
WROWS = F // N_REP
PA = 176
PD = 160
QA = XR - PA
QD = XR - PD
T_CHUNKS = 8
UNROLL = 4

f32 = jnp.float32
bf16 = jnp.bfloat16
VMEM_LIMIT = 56 << 20


def pair_swap(x, axis):
    return lax.ppermute(x, axis, [(0, 1), (1, 0)])


def spread(x, axes, n):
    return lax.all_to_all(jnp.broadcast_to(x[None], (n,) + x.shape), axes, 0, 0, tiled=True)


def slot_loop(count, wait_chunk, one_slot):
    per_chunk = SLOTS // T_CHUNKS
    for chunk in range(T_CHUNKS):
        wait_chunk(chunk)
        left = jnp.clip(count - chunk * per_chunk, 0, per_chunk)

        def step(i, carry, base=chunk * per_chunk):
            for u in range(UNROLL):
                one_slot(base + i * UNROLL + u)
            return carry

        lax.fori_loop(0, (left + UNROLL - 1) // UNROLL, step, 0)


def tile_copies(tiles_hbm, tiles, sems, first):
    per_chunk = SLOTS // T_CHUNKS
    return [
        pltpu.make_async_copy(
            tiles_hbm.at[pl.ds(c * per_chunk, per_chunk)],
            tiles.at[pl.ds(c * per_chunk, per_chunk)],
            sems.at[first + c],
        )
        for c in range(T_CHUNKS)
    ]


def forward_kernel(rows, slots, count, tiles_hbm, p00, p01, p10, p11, q0, q1, out, x, tiles, acc, sems):
    copies = []
    for v, src in enumerate((p00, p01, p10, p11)):
        copies.append(pltpu.make_async_copy(src, x.at[pl.ds(v * N_Z, N_Z), pl.ds(0, PA)], sems.at[v]))
    for dc, src in enumerate((q0, q1)):
        for dx in range(2):
            v = 2 * dx + dc
            copies.append(
                pltpu.make_async_copy(
                    src.at[:, pl.ds(dx * QA, QA)], x.at[pl.ds(v * N_Z, N_Z), pl.ds(PA, QA)], sems.at[4 + v]
                )
            )
    tile_in = tile_copies(tiles_hbm, tiles, sems, 8)
    for c in copies:
        c.start()
    for c in tile_in:
        c.start()
    acc[...] = jnp.zeros_like(acc)
    for c in copies:
        c.wait()

    def one_slot(t):
        s = slots[t]
        row = rows[t]
        feats = x[s >> 1, pl.ds(pl.multiple_of((s & 1) * TILE, TILE), TILE), :]
        acc[row] += jnp.dot(tiles[t], feats, preferred_element_type=f32)

    slot_loop(count[0], lambda c: tile_in[c].wait(), one_slot)
    for r in range(N_REP):
        for h in range(2):
            out[r, pl.ds(h * TILE, TILE), :] = acc[2 * r + h].astype(bf16)


def backward_kernel(rows, slots, count, tiles_hbm, grads_hbm, p00, p01, p10, p11, q0, q1, grads, tiles, acc, sems):
    grads_in = pltpu.make_async_copy(grads_hbm.at[:, pl.ds(0, XR)], grads, sems.at[0])
    tile_in = tile_copies(tiles_hbm, tiles, sems, 1)
    grads_in.start()
    for c in tile_in:
        c.start()
    acc[...] = jnp.zeros_like(acc)
    grads_in.wait()

    def one_slot(t):
        s = slots[t]
        row = rows[t]
        here = (s >> 1, pl.ds(pl.multiple_of((s & 1) * TILE, TILE), TILE))
        g = grads[row >> 1, pl.ds(pl.multiple_of((row & 1) * TILE, TILE), TILE), :]
        acc[here[0], here[1], :] += lax.dot_general(
            tiles[t], g, (((0,), (0,)), ((), ())), preferred_element_type=f32
        )

    slot_loop(count[0], lambda c: tile_in[c].wait(), one_slot)
    for v, out in enumerate((p00, p01, p10, p11)):
        for z in range(N_Z):
            out[z] = acc[v * N_Z + z, pl.ds(0, PD), :].astype(bf16)
    for dc, out in enumerate((q0, q1)):
        for dx in range(2):
            for z in range(N_Z):
                out[z, pl.ds(dx * QD, QD), :] = acc[(2 * dx + dc) * N_Z + z, pl.ds(PD, QD), :].astype(bf16)


def dense_kernel(parts, weight, cot, layer_out, payload):
    total = parts[0].astype(f32)
    for r in range(1, N_REP):
        total += parts[r].astype(f32)
    hidden = total.astype(bf16)
    w = weight[...]
    preact = jnp.dot(hidden, w, preferred_element_type=f32)
    gating = jax.nn.sigmoid(preact)
    layer_out[...] = (preact * gating).astype(bf16)
    slope = gating * (1.0 + preact * (1.0 - gating))
    grad_pre = (cot[...].astype(f32) * slope).astype(bf16)
    grad_hidden = lax.dot_general(grad_pre, w, (((1,), (1,)), ((), ())), preferred_element_type=f32).astype(bf16)
    weight_part = lax.dot_general(hidden, grad_pre, (((0,), (0,)), ((), ())), preferred_element_type=f32).astype(bf16)
    for r in range(N_REP):
        payload[r, pl.ds(0, XR), :] = grad_hidden
        payload[r, pl.ds(XR, WROWS), :] = weight_part[r * WROWS : (r + 1) * WROWS]


def on_device(node_features, tile_values, tile_row, tile_col, tile_count, weight, cotangent):
    sds = jax.ShapeDtypeStruct
    smem = pl.BlockSpec(memory_space=pltpu.SMEM)
    hbm = pl.BlockSpec(memory_space=pl.ANY)
    params = pltpu.CompilerParams(vmem_limit_bytes=VMEM_LIMIT)
    tiles = tile_values[0, 0]
    count = tile_count[0]
    cols = tile_col[0, 0]
    my_xl = lax.axis_index("xl")
    my_core = lax.axis_index("core")
    owner = cols >> 1
    variant = 2 * (((owner >> 1) & 1) ^ my_xl) + ((owner & 1) ^ my_core)
    slots = ((variant * N_Z + (owner >> 2)) << 1) | (cols & 1)
    live = jnp.arange(SLOTS, dtype=jnp.int32) < count[0]
    rows_fwd = jnp.where(live, tile_row[0, 0], ROW_BLOCKS)
    slots_bwd = jnp.where(live, slots, 8 * N_Z)

    own_p = node_features[:PA]
    own_q = node_features[PA:]
    with jax.named_scope("gather_features"):
        other_q = pair_swap(own_q, "xl")
        p00 = spread(own_p, "z", N_Z)
        q0 = spread(jnp.concatenate([own_q, other_q], axis=0), "z", N_Z)
        p10 = pair_swap(p00, "xl")
        p01 = pair_swap(p00, "core")
        q1 = pair_swap(q0, "core")
        p11 = pair_swap(p10, "core")
    with jax.named_scope("tile_products"):
        partial = pl.pallas_call(
            forward_kernel,
            out_shape=sds((N_REP, XR, F), bf16),
            in_specs=[smem, smem, smem] + [hbm] * 7,
            scratch_shapes=[
                pltpu.VMEM((4 * N_Z, XR, F), bf16),
                pltpu.VMEM((SLOTS, TILE, TILE), bf16),
                pltpu.VMEM((ROW_BLOCKS + 1, TILE, F), f32),
                pltpu.SemaphoreType.DMA((8 + T_CHUNKS,)),
            ],
            compiler_params=params,
            name="tile_products",
        )(rows_fwd, slots, count, tiles, p00, p01, p10, p11, q0, q1)
    with jax.named_scope("sum_partials"):
        parts = lax.all_to_all(partial, REP, 0, 0, tiled=True)
    with jax.named_scope("dense"):
        layer_out, payload = pl.pallas_call(
            dense_kernel,
            out_shape=(sds((XR, F), bf16), sds((N_REP, XR + WROWS, F), bf16)),
            compiler_params=params,
            name="dense",
        )(parts, weight, cotangent[0, 0])
    with jax.named_scope("share_gradients"):
        grads = lax.all_to_all(payload, REP, 0, 0, tiled=True)
    with jax.named_scope("weight_sum"):
        w = jnp.sum(grads[:, XR:, :].astype(f32), axis=0)
        w = w + pair_swap(w, "core")
        w = w + pair_swap(w, "xl")
    with jax.named_scope("tile_products_back"):
        p00, p01, p10, p11, q0, q1 = pl.pallas_call(
            backward_kernel,
            out_shape=[sds((N_Z, PD, F), bf16)] * 4 + [sds((N_Z, 2 * QD, F), bf16)] * 2,
            in_specs=[smem, smem, smem] + [hbm] * 2,
            scratch_shapes=[
                pltpu.VMEM((N_REP, XR, F), bf16),
                pltpu.VMEM((SLOTS, TILE, TILE), bf16),
                pltpu.VMEM((4 * N_Z + 1, XR, F), f32),
                pltpu.SemaphoreType.DMA((1 + T_CHUNKS,)),
            ],
            compiler_params=params,
            name="tile_products_back",
        )(tile_row[0, 0], slots_bwd, count, tiles, grads)
    with jax.named_scope("scatter_gradients"):
        r10 = pair_swap(p11, "core")
        rq = pair_swap(q1, "core")
        r00 = pair_swap(p01, "core")
        far = pair_swap((p10.astype(f32) + r10.astype(f32)).astype(bf16), "xl")
        qz = lax.all_to_all((q0.astype(f32) + rq.astype(f32)).astype(bf16), "z", 0, 0, tiled=True)
        near = (p00.astype(f32) + r00.astype(f32) + far.astype(f32)).astype(bf16)
        pz = lax.all_to_all(near, "z", 0, 0, tiled=True)
        q_sum = jnp.sum(qz.astype(f32), axis=0)
        q_far = pair_swap(q_sum[QD:].astype(bf16), "xl")
        q_out = (q_sum[:QD] + q_far.astype(f32)).astype(bf16)
        p_out = jnp.sum(pz.astype(f32), axis=0).astype(bf16)
        grad_features = jnp.concatenate([p_out, q_out], axis=0)
    with jax.named_scope("weight_sum"):
        w = jnp.sum(spread(w, "z", N_Z), axis=0)
        grad_weight = spread(w, REP, N_REP).reshape(F, F)
    return layer_out.reshape(1, 1, XR, F), grad_weight, grad_features


def solution(mesh):
    fine = Mesh(np.asarray(mesh.devices).reshape(4, 2, 8, 2, 2), REP + BLK)
    placed = (
        P(REP + BLK, None),
        P(REP, BLK, None, None, None),
        P(REP, BLK, None),
        P(REP, BLK, None),
        P(REP, BLK),
        P(),
        P(BLK, REP, None, None),
    )
    return jax.shard_map(
        on_device,
        mesh=fine,
        in_specs=placed,
        out_specs=(P(BLK, REP, None, None), P(), P(REP + BLK, None)),
        check_vma=False,
    )
```

```python
import jax
import jax.numpy as jnp
import numpy as np
from jax import lax
from jax.experimental import pallas as pl
from jax.experimental.pallas import tpu as pltpu
from jax.sharding import Mesh
from jax.sharding import PartitionSpec as P

REP = ("y", "xh")
BLK = ("z", "xl", "core")
PLANE = ("z", "xl")
N_PLANE = 16
N_Z = 8
N_Y = 4
TILE = 128
F = 256
XR = 256
N_REP = 8
SLOTS = 128
ROW_BLOCKS = 16
WROWS = F // N_REP
UNROLL = 4

f32 = jnp.float32
bf16 = jnp.bfloat16
VMEM_LIMIT = 24 << 20


def xor_swap(x, axis, n, bit):
    return lax.ppermute(x, axis, [(i, i ^ bit) for i in range(n)])


def half(ref, i):
    return ref[i >> 1, pl.ds(pl.multiple_of((i & 1) * TILE, TILE), TILE), :]


def slot_loop(table, side, one_slot):
    live = table[6, side]

    def step(i, carry):
        for u in range(UNROLL):
            t = i * UNROLL + u
            one_slot(t < live, table[3 * side, t], table[3 * side + 1, t], table[3 * side + 2, t])
        return carry

    lax.fori_loop(0, (live + UNROLL - 1) // UNROLL, step, 0)


def add_products(table, side, tiles, feats, acc):
    acc[...] = jnp.zeros_like(acc)

    def one_slot(ok, row, place, tile):
        r = jnp.where(ok, row, ROW_BLOCKS)
        acc[r] += jnp.dot(tiles[tile], half(feats, place), preferred_element_type=f32)

    slot_loop(table, side, one_slot)


def forward_near_kernel(table, tiles, feats, acc):
    add_products(table, 0, tiles, feats, acc)


def forward_far_kernel(table, tiles, feats, near, out, acc):
    add_products(table, 1, tiles, feats, acc)
    for r in range(N_REP):
        for h in range(2):
            out[r, pl.ds(h * TILE, TILE), :] = (near[2 * r + h] + acc[2 * r + h]).astype(bf16)


def backward_kernel(side, table, tiles, grads, out, acc):
    acc[...] = jnp.zeros_like(acc)

    def one_slot(ok, row, place, tile):
        p = jnp.where(ok, place, 2 * N_PLANE)
        acc[p] += lax.dot_general(
            tiles[tile], half(grads, row), (((0,), (0,)), ((), ())), preferred_element_type=f32
        )

    slot_loop(table, side, one_slot)
    for k in range(N_PLANE):
        for h in range(2):
            out[k, pl.ds(h * TILE, TILE), :] = acc[2 * k + h].astype(bf16)


def dense_kernel(parts, weight, cot, layer_out, payload):
    total = parts[0].astype(f32)
    for r in range(1, N_REP):
        total += parts[r].astype(f32)
    hidden = total.astype(bf16)
    w = weight[...]
    preact = jnp.dot(hidden, w, preferred_element_type=f32)
    gating = jax.nn.sigmoid(preact)
    layer_out[...] = (preact * gating).astype(bf16)
    slope = gating * (1.0 + preact * (1.0 - gating))
    grad_pre = (cot[...].astype(f32) * slope).astype(bf16)
    grad_hidden = lax.dot_general(grad_pre, w, (((1,), (1,)), ((), ())), preferred_element_type=f32).astype(bf16)
    weight_part = lax.dot_general(hidden, grad_pre, (((0,), (0,)), ((), ())), preferred_element_type=f32).astype(bf16)
    for r in range(N_REP):
        payload[r, pl.ds(0, XR), :] = grad_hidden
        payload[r, pl.ds(XR, WROWS), :] = weight_part[r * WROWS : (r + 1) * WROWS]


def slot_table(rows, cols, count, my_core):
    owner = cols >> 1
    place = ((owner >> 1) << 1) | (cols & 1)
    position = jnp.arange(SLOTS, dtype=jnp.int32)
    live = position < count
    far = (owner & 1) != my_core
    lists = []
    totals = []
    for side in (live & ~far, live & far):
        rank = jnp.cumsum(side.astype(jnp.int32)) - 1
        pick = (side[None, :] & (rank[None, :] == position[:, None])).astype(jnp.int32)
        for values in (rows, place, position):
            lists.append(jnp.sum(pick * values[None, :], axis=1))
        totals.append(jnp.sum(side.astype(jnp.int32)))
    last = jnp.where(position == 0, totals[0], jnp.where(position == 1, totals[1], 0))
    return jnp.stack(lists + [last, jnp.zeros_like(last)])


def on_device(node_features, tile_values, tile_row, tile_col, tile_count, weight, cotangent):
    sds = jax.ShapeDtypeStruct
    smem = pl.BlockSpec(memory_space=pltpu.SMEM)
    vmem = pl.BlockSpec(memory_space=pltpu.VMEM)
    params = pltpu.CompilerParams(vmem_limit_bytes=VMEM_LIMIT)
    tiles = tile_values[0, 0]
    my_core = lax.axis_index("core")

    with jax.named_scope("slot_table"):
        table = slot_table(tile_row[0, 0], tile_col[0, 0], tile_count[0, 0], my_core)
    with jax.named_scope("gather_features"):
        near_feats = lax.all_to_all(
            jnp.broadcast_to(node_features[None], (N_PLANE, XR, F)), PLANE, 0, 0, tiled=True
        )
        near_feats, table = lax.optimization_barrier((near_feats, table))
        far_feats = xor_swap(near_feats, "core", 2, 1)
    with jax.named_scope("tile_products"):
        near = pl.pallas_call(
            forward_near_kernel,
            out_shape=sds((ROW_BLOCKS + 1, TILE, F), f32),
            in_specs=[smem, vmem, vmem],
            out_specs=vmem,
            compiler_params=params,
            name="tile_products_near",
        )(table, tiles, near_feats)
        partial = pl.pallas_call(
            forward_far_kernel,
            out_shape=sds((N_REP, XR, F), bf16),
            in_specs=[smem, vmem, vmem, vmem],
            out_specs=vmem,
            scratch_shapes=[pltpu.VMEM((ROW_BLOCKS + 1, TILE, F), f32)],
            compiler_params=params,
            name="tile_products_far",
        )(table, tiles, far_feats, near)
    with jax.named_scope("sum_partials"):
        parts = lax.all_to_all(partial, REP, 0, 0, tiled=True)
    with jax.named_scope("dense"):
        layer_out, payload = pl.pallas_call(
            dense_kernel,
            out_shape=(sds((XR, F), bf16), sds((N_REP, XR + WROWS, F), bf16)),
            in_specs=[vmem] * 3,
            out_specs=[vmem] * 2,
            compiler_params=params,
            name="dense",
        )(parts, weight, cotangent[0, 0])
    with jax.named_scope("share_gradients"):
        grads = lax.all_to_all(payload, REP, 0, 0, tiled=True)

    def backward(side, name):
        return pl.pallas_call(
            lambda *refs: backward_kernel(side, *refs),
            out_shape=sds((N_PLANE, XR, F), bf16),
            in_specs=[smem, vmem, vmem],
            out_specs=vmem,
            scratch_shapes=[pltpu.VMEM((2 * N_PLANE + 1, TILE, F), f32)],
            compiler_params=params,
            name=name,
        )(table, tiles, grads)

    with jax.named_scope("tile_products_back"):
        far_back = backward(1, "tile_products_back_far")
        from_core = xor_swap(far_back, "core", 2, 1)
        near_back = backward(0, "tile_products_back_near")
        back = (near_back.astype(f32) + from_core.astype(f32)).astype(bf16)
    with jax.named_scope("scatter_gradients"):
        returned = lax.all_to_all(back, PLANE, 0, 0, tiled=True)
        grad_features = jnp.sum(returned.astype(f32), axis=0).astype(bf16)
    with jax.named_scope("weight_sum"):
        terms, _ = lax.optimization_barrier((grads[:, XR:, :], back))
        w = jnp.sum(terms.astype(f32), axis=0)
        w = w + xor_swap(w, "core", 2, 1)
        w = w + xor_swap(w, "xl", 2, 1)
        for bit in (1, 2, 4):
            w = w + xor_swap(w, "z", N_Z, bit)
        for axis, n, bit in (("xh", 2, 1), ("y", N_Y, 1), ("y", N_Y, 2)):
            other = xor_swap(w, axis, n, bit)
            upper = (lax.axis_index(axis) & bit) != 0
            w = jnp.where(upper, jnp.concatenate([other, w], axis=0), jnp.concatenate([w, other], axis=0))
    return layer_out.reshape(1, 1, XR, F), w, grad_features


def solution(mesh):
    fine = Mesh(np.asarray(mesh.devices).reshape(N_Y, 2, N_Z, 2, 2), REP + BLK)
    placed = (
        P(REP + BLK, None),
        P(REP, BLK, None, None, None),
        P(REP, BLK, None),
        P(REP, BLK, None),
        P(REP, BLK),
        P(),
        P(BLK, REP, None, None),
    )
    return jax.shard_map(
        on_device,
        mesh=fine,
        in_specs=placed,
        out_specs=(P(BLK, REP, None, None), P(), P(REP + BLK, None)),
        check_vma=False,
    )
```

```python
import jax
import jax.numpy as jnp
import numpy as np
from jax import lax
from jax.experimental import pallas as pl
from jax.experimental.pallas import tpu as pltpu
from jax.sharding import Mesh
from jax.sharding import PartitionSpec as P

REP = ("y", "xh")
BLK = ("z", "xl", "core")
N_Z = 8
N_Y = 4
TILE = 128
F = 256
XR = 256
N_REP = 8
SLOTS = 128
ROW_BLOCKS = 16
UNROLL = 4
CLASSES = 6

f32 = jnp.float32
bf16 = jnp.bfloat16
VMEM_LIMIT = 12 << 20


def xor_swap(x, axis, n, bit):
    return lax.ppermute(x, axis, [(i, i ^ bit) for i in range(n)])


def add_swapped(x, axis, n, bit):
    return (x.astype(f32) + xor_swap(x, axis, n, bit).astype(f32)).astype(bf16)


def slot_table(rows, cols, count, my_xl, my_core):
    owner = cols >> 1
    z = owner >> 2
    dx = ((owner >> 1) & 1) ^ my_xl
    dc = (owner & 1) ^ my_core
    second = (cols & 1) == 1
    position = jnp.arange(SLOTS, dtype=jnp.int32)
    kind = jnp.where(position < count, jnp.where(second, 4 + dc, 2 * dc + dx), CLASSES)
    place = jnp.where(second, z * 2 + dx, dx * N_Z + z)
    packed = rows | (place << 8) | (position << 16)
    key = kind * SLOTS + position
    rank = jnp.sum((key[None, :] < key[:, None]).astype(jnp.int32), axis=1)
    ordered = jnp.sum(jnp.where(rank[None, :] == position[:, None], packed[None, :], 0), axis=1)
    starts = jnp.sum((kind[None, :] < position[:, None]).astype(jnp.int32), axis=1)
    return jnp.concatenate([jnp.stack([ordered, starts]), jnp.zeros((2, SLOTS), jnp.int32)], axis=1)


def slot_range(table, first, last):
    return table[1, first], table[1, last]


def tile_copy(table, tiles_hbm, tiles, sems, t):
    return pltpu.make_async_copy(tiles_hbm.at[table[0, t] >> 16], tiles.at[t], sems.at[t])


def start_tiles(table, first, last, tiles_hbm, tiles, sems):
    begin, end = slot_range(table, first, last)

    def start(t, carry):
        tile_copy(table, tiles_hbm, tiles, sems, t).start()
        return carry

    lax.fori_loop(begin, end, start, 0)


def slot_loop(table, first, last, tiles_hbm, tiles, sems, one_slot):
    begin, end = slot_range(table, first, last)

    def several(n):
        def step(i, carry):
            t0 = carry
            for u in range(n):
                tile_copy(table, tiles_hbm, tiles, sems, t0 + u).wait()
            for u in range(n):
                packed = table[0, t0 + u]
                one_slot(t0 + u, packed & 255, (packed >> 8) & 255)
            return t0 + n

        return step

    rounds = (end - begin) // UNROLL
    t0 = lax.fori_loop(0, rounds, several(UNROLL), begin)
    lax.fori_loop(0, end - begin - rounds * UNROLL, several(1), t0)


def add_products(table, first, tiles_hbm, feats, mask, acc, tiles, sems):
    def one_slot(t, row, place):
        acc[row] += jnp.dot(tiles[t], feats[place & mask], preferred_element_type=f32)

    slot_loop(table, first, first + 1, tiles_hbm, tiles, sems, one_slot)


def forward_first_kernel(table, tiles_hbm, near0, near1, far0, far1, acc, tiles, sems):
    start_tiles(table, 0, 4, tiles_hbm, tiles, sems)
    acc[...] = jnp.zeros_like(acc)
    for k, feats in enumerate((near0, near1, far0, far1)):
        add_products(table, k, tiles_hbm, feats, N_Z - 1, acc, tiles, sems)


def forward_second_kernel(table, tiles_hbm, feats, before, acc, tiles, sems):
    start_tiles(table, 4, 5, tiles_hbm, tiles, sems)
    acc[...] = before[...]
    add_products(table, 4, tiles_hbm, feats, 2 * N_Z - 1, acc, tiles, sems)


def forward_last_kernel(table, tiles_hbm, feats, before, out, tiles, sems, acc):
    start_tiles(table, 5, 6, tiles_hbm, tiles, sems)
    acc[...] = before[...]
    add_products(table, 5, tiles_hbm, feats, 2 * N_Z - 1, acc, tiles, sems)
    for r in range(N_REP):
        for h in range(2):
            out[r, pl.ds(h * TILE, TILE), :] = acc[2 * r + h].astype(bf16)


def backward_kernel(first, last, table, tiles_hbm, grads, out, tiles, sems, acc):
    start_tiles(table, first, last, tiles_hbm, tiles, sems)
    acc[...] = jnp.zeros_like(acc)

    def one_slot(t, row, place):
        g = grads[row >> 1, pl.ds(pl.multiple_of((row & 1) * TILE, TILE), TILE), :]
        acc[place] += lax.dot_general(tiles[t], g, (((0,), (0,)), ((), ())), preferred_element_type=f32)

    slot_loop(table, first, last, tiles_hbm, tiles, sems, one_slot)
    for k in range(2 * N_Z):
        out[k] = acc[k].astype(bf16)


def dense_kernel(parts, weight, cot, layer_out, payload, weight_part):
    total = parts[0].astype(f32)
    for r in range(1, N_REP):
        total += parts[r].astype(f32)
    hidden = total.astype(bf16)
    w = weight[...]
    preact = jnp.dot(hidden, w, preferred_element_type=f32)
    gating = jax.nn.sigmoid(preact)
    layer_out[...] = (preact * gating).astype(bf16)
    slope = gating * (1.0 + preact * (1.0 - gating))
    grad_pre = (cot[...].astype(f32) * slope).astype(bf16)
    grad_hidden = lax.dot_general(grad_pre, w, (((1,), (1,)), ((), ())), preferred_element_type=f32).astype(bf16)
    for r in range(N_REP):
        payload[r] = grad_hidden
    weight_part[...] = lax.dot_general(
        hidden, grad_pre, (((0,), (0,)), ((), ())), preferred_element_type=f32
    ).astype(bf16)


def on_device(node_features, tile_values, tile_row, tile_col, tile_count, weight, cotangent):
    sds = jax.ShapeDtypeStruct
    smem = pl.BlockSpec(memory_space=pltpu.SMEM)
    vmem = pl.BlockSpec(memory_space=pltpu.VMEM)
    params = pltpu.CompilerParams(vmem_limit_bytes=VMEM_LIMIT)
    acc_rows = sds((ROW_BLOCKS, TILE, F), f32)
    hbm = pl.BlockSpec(memory_space=pltpu.HBM)
    tile_room = [pltpu.VMEM((SLOTS, TILE, TILE), bf16), pltpu.SemaphoreType.DMA((SLOTS,))]
    tiles = pltpu.with_memory_space_constraint(tile_values[0, 0], pltpu.HBM)
    my_core = lax.axis_index("core")
    my_xl = lax.axis_index("xl")

    def call(kernel, name, out_shape, *args, scratch=()):
        return pl.pallas_call(
            kernel,
            out_shape=out_shape,
            in_specs=[smem, hbm] + [vmem] * (len(args) - 2),
            out_specs=vmem,
            scratch_shapes=tile_room + list(scratch),
            compiler_params=params,
            cost_estimate=pl.CostEstimate(flops=1, transcendentals=0, bytes_accessed=1),
            name=name,
        )(*args)

    with jax.named_scope("slot_table"):
        table = slot_table(tile_row[0, 0], tile_col[0, 0], tile_count[0, 0], my_xl, my_core)
    with jax.named_scope("gather_features"):
        first = jnp.broadcast_to(node_features[None, :TILE], (N_Z, TILE, F))
        near0 = lax.all_to_all(first, "z", 0, 0, tiled=True)
        own = node_features[TILE:]
        other = xor_swap(own, "xl", 2, 1)
        pair = jnp.broadcast_to(jnp.stack([own, other])[None], (N_Z, 2, TILE, F))
        near0, pair, table = lax.optimization_barrier((near0, pair, table))
        near_pair = lax.all_to_all(pair, "z", 0, 0, tiled=True).reshape(2 * N_Z, TILE, F)
        near1 = xor_swap(near0, "xl", 2, 1)
        far0 = xor_swap(near0, "core", 2, 1)
        far1 = xor_swap(near1, "core", 2, 1)
    with jax.named_scope("tile_products"):
        acc = call(forward_first_kernel, "tile_products_first", acc_rows, table, tiles, near0, near1, far0, far1)
        near_pair, acc = lax.optimization_barrier((near_pair, acc))
        far_pair = xor_swap(near_pair, "core", 2, 1)
        acc = call(forward_second_kernel, "tile_products_second", acc_rows, table, tiles, near_pair, acc)
        partial = call(
            forward_last_kernel,
            "tile_products_last",
            sds((N_REP, XR, F), bf16),
            table,
            tiles,
            far_pair,
            acc,
            scratch=[pltpu.VMEM((ROW_BLOCKS, TILE, F), f32)],
        )
    with jax.named_scope("sum_partials"):
        parts = lax.all_to_all(partial, REP, 0, 0, tiled=True)
    with jax.named_scope("dense"):
        layer_out, payload, weight_part = pl.pallas_call(
            dense_kernel,
            out_shape=(sds((XR, F), bf16), sds((N_REP, XR, F), bf16), sds((F, F), bf16)),
            in_specs=[vmem] * 3,
            out_specs=[vmem] * 3,
            compiler_params=params,
            name="dense",
        )(parts, weight, cotangent[0, 0])
    with jax.named_scope("share_gradients"):
        grads = lax.all_to_all(payload, REP, 0, 0, tiled=True)
    with jax.named_scope("weight_z"):
        w = weight_part
        for bit in (1, 2, 4):
            w = add_swapped(w, "z", N_Z, bit)
        grads, w = lax.optimization_barrier((grads, w))

    def backward(first, last, name):
        return call(
            lambda *refs: backward_kernel(first, last, *refs),
            name,
            sds((2 * N_Z, TILE, F), bf16),
            table,
            tiles,
            grads,
            scratch=[pltpu.VMEM((2 * N_Z, TILE, F), f32)],
        )

    with jax.named_scope("back_second"):
        far_back = backward(5, 6, "back_second_far")
        got = xor_swap(far_back, "core", 2, 1)
        near_back = backward(4, 5, "back_second_near")
        pair = (near_back.astype(f32) + got.astype(f32)).astype(bf16)
        pair, table, w = lax.optimization_barrier((pair, table, w))
        pair_got = lax.all_to_all(pair.reshape(N_Z, 2, TILE, F), "z", 0, 0, tiled=True)
    with jax.named_scope("back_first"):
        far_back = backward(2, 4, "back_first_far")
        got = xor_swap(far_back, "core", 2, 1)
        near_back = backward(0, 2, "back_first_near")
        away = (near_back[N_Z:].astype(f32) + got[N_Z:].astype(f32)).astype(bf16)
        back = xor_swap(away, "xl", 2, 1)
        for bit in (1, 2):
            w = add_swapped(w, "y", N_Y, bit)
        home = (near_back[:N_Z].astype(f32) + got[:N_Z].astype(f32) + back.astype(f32)).astype(bf16)
        home, w = lax.optimization_barrier((home, w))
        home_got = lax.all_to_all(home, "z", 0, 0, tiled=True)
    with jax.named_scope("grad_features"):
        pair_sum = jnp.sum(pair_got.astype(f32), axis=0)
        back = xor_swap(pair_sum[1].astype(bf16), "xl", 2, 1)
        second_sum = (pair_sum[0] + back.astype(f32)).astype(bf16)
        first_sum = jnp.sum(home_got.astype(f32), axis=0).astype(bf16)
        grad_features = jnp.concatenate([first_sum, second_sum], axis=0)
    with jax.named_scope("weight_rest"):
        w, _ = lax.optimization_barrier((w, pair_sum))
        w = add_swapped(w, "xl", 2, 1)
        w = add_swapped(w, "xh", 2, 1)
        grad_weight = w.astype(f32) + xor_swap(w, "core", 2, 1).astype(f32)
    return layer_out.reshape(1, 1, XR, F), grad_weight, grad_features


def solution(mesh):
    fine = Mesh(np.asarray(mesh.devices).reshape(N_Y, 2, N_Z, 2, 2), REP + BLK)
    placed = (
        P(REP + BLK, None),
        P(REP, BLK, None, None, None),
        P(REP, BLK, None),
        P(REP, BLK, None),
        P(REP, BLK),
        P(),
        P(BLK, REP, None, None),
    )
    return jax.shard_map(
        on_device,
        mesh=fine,
        in_specs=placed,
        out_specs=(P(BLK, REP, None, None), P(), P(REP + BLK, None)),
        check_vma=False,
    )
```

```python
import jax
import jax.numpy as jnp
import numpy as np
from jax import lax
from jax.experimental import pallas as pl
from jax.experimental.pallas import tpu as pltpu
from jax.sharding import Mesh
from jax.sharding import PartitionSpec as P

REP = ("y", "xh")
BLK = ("z", "xl", "core")
N_Z = 8
N_Y = 4
TILE = 128
F = 256
XR = 256
N_REP = 8
SLOTS = 128
ROW_BLOCKS = 16
UNROLL = 8
CLASSES = 6

f32 = jnp.float32
bf16 = jnp.bfloat16
VMEM_LIMIT = 16 << 20


def xor_swap(x, axis, n, bit):
    return lax.ppermute(x, axis, [(i, i ^ bit) for i in range(n)])


def add_swapped(x, axis, n, bit):
    return (x.astype(f32) + xor_swap(x, axis, n, bit).astype(f32)).astype(bf16)


def hold(operand, value):
    return lax.optimization_barrier((operand.reshape(-1, F)[:16], value))


def slot_table(rows, cols, count, my_xl, my_core):
    owner = cols >> 1
    z = owner >> 2
    dx = ((owner >> 1) & 1) ^ my_xl
    dc = (owner & 1) ^ my_core
    second = (cols & 1) == 1
    position = jnp.arange(SLOTS, dtype=jnp.int32)
    kind = jnp.where(position < count, jnp.where(second, 4 + dc, 2 * dc + dx), CLASSES)
    place = jnp.where(second, z * 2 + dx, dx * N_Z + z)
    packed = rows | (place << 8) | (position << 16)
    key = kind * SLOTS + position
    rank = jnp.sum((key[None, :] < key[:, None]).astype(jnp.int32), axis=1)
    ordered = jnp.sum(jnp.where(rank[None, :] == position[:, None], packed[None, :], 0), axis=1)
    starts = jnp.sum((kind[None, :] < position[:, None]).astype(jnp.int32), axis=1)
    return jnp.concatenate([jnp.stack([ordered, starts]), jnp.zeros((2, SLOTS), jnp.int32)], axis=1)


def slot_range(table, first, last):
    begin = table[1, first]
    return begin, (table[1, last] - begin + UNROLL - 1) // UNROLL


def start_tiles(table, first, last, tiles_hbm, tiles, sems):
    begin, rounds = slot_range(table, first, last)

    def start(i, carry):
        for u in range(UNROLL):
            at = i * UNROLL + u
            pltpu.make_async_copy(tiles_hbm.at[table[0, begin + at] >> 16], tiles.at[at], sems.at[i]).start()
        return carry

    lax.fori_loop(0, rounds, start, 0)


def slot_loop(table, first, last, tiles_hbm, tiles, sems, one_slot):
    begin, rounds = slot_range(table, first, last)
    end = table[1, last]

    def step(i, carry):
        pltpu.make_async_copy(
            tiles_hbm.at[pl.ds(0, UNROLL)], tiles.at[pl.ds(i * UNROLL, UNROLL)], sems.at[i]
        ).wait()
        for u in range(UNROLL):
            t = begin + i * UNROLL + u
            packed = table[0, t]
            one_slot(t < end, packed & 255, (packed >> 8) & 255, tiles[i * UNROLL + u])
        return carry

    lax.fori_loop(0, rounds, step, 0)


def add_products(table, first, feats, mask, acc, room):
    def one_slot(live, row, place, tile):
        target = jnp.where(live, row, ROW_BLOCKS)
        acc[target] += jnp.dot(tile, feats[place & mask], preferred_element_type=f32)

    slot_loop(table, first, first + 1, *room, one_slot)


def forward_first_kernel(table, tiles_hbm, near0, near1, far0, far1, acc, tiles, sems):
    begin = table[1, 0]
    start_tiles(table, 0, 4, tiles_hbm, tiles, sems)
    acc[...] = jnp.zeros_like(acc)
    _, rounds = slot_range(table, 0, 4)

    def wait(i, carry):
        pltpu.make_async_copy(
            tiles_hbm.at[pl.ds(0, UNROLL)], tiles.at[pl.ds(i * UNROLL, UNROLL)], sems.at[i]
        ).wait()
        return carry

    lax.fori_loop(0, rounds, wait, 0)
    for k, feats in enumerate((near0, near1, far0, far1)):
        first, steps = slot_range(table, k, k + 1)
        end = table[1, k + 1]

        def step(i, carry):
            for u in range(UNROLL):
                t = first + i * UNROLL + u
                packed = table[0, t]
                target = jnp.where(t < end, packed & 255, ROW_BLOCKS)
                at = jnp.minimum(t - begin, SLOTS - 1)
                acc[target] += jnp.dot(
                    tiles[at], feats[(packed >> 8) & (N_Z - 1)], preferred_element_type=f32
                )
            return carry

        lax.fori_loop(0, steps, step, 0)


def forward_second_kernel(table, tiles_hbm, feats, before, acc, tiles, sems):
    start_tiles(table, 4, 5, tiles_hbm, tiles, sems)
    acc[...] = before[...]
    add_products(table, 4, feats, 2 * N_Z - 1, acc, (tiles_hbm, tiles, sems))


def forward_last_kernel(table, tiles_hbm, feats, before, out, tiles, sems, acc):
    start_tiles(table, 5, 6, tiles_hbm, tiles, sems)
    acc[...] = before[...]
    add_products(table, 5, feats, 2 * N_Z - 1, acc, (tiles_hbm, tiles, sems))
    for r in range(N_REP):
        for h in range(2):
            out[r, pl.ds(h * TILE, TILE), :] = acc[2 * r + h].astype(bf16)


def backward_kernel(ranges, table, tiles_hbm, grads, *rest):
    tiles, sems, acc = rest[-3:]
    outs = rest[-3 - len(ranges) : -3]
    for n, (first, last) in enumerate(ranges):
        start_tiles(table, first, last, tiles_hbm, tiles.at[n], sems.at[n])
    for n, ((first, last), out) in enumerate(zip(ranges, outs)):
        acc[...] = jnp.zeros_like(acc)

        def one_slot(live, row, place, tile):
            target = jnp.where(live, place, 2 * N_Z)
            g = grads[row >> 1, pl.ds(pl.multiple_of((row & 1) * TILE, TILE), TILE), :]
            acc[target] += lax.dot_general(tile, g, (((0,), (0,)), ((), ())), preferred_element_type=f32)

        slot_loop(table, first, last, tiles_hbm, tiles.at[n], sems.at[n], one_slot)
        for k in range(2 * N_Z):
            out[k] = acc[k].astype(bf16)


def final_weight_kernel(mine, other, small, out):
    out[...] = mine[...].astype(f32) + other[...].astype(f32)


def dense_kernel(parts, weight, cot, layer_out, payload, weight_part):
    total = parts[0].astype(f32)
    for r in range(1, N_REP):
        total += parts[r].astype(f32)
    hidden = total.astype(bf16)
    w = weight[...]
    preact = jnp.dot(hidden, w, preferred_element_type=f32)
    gating = jax.nn.sigmoid(preact)
    layer_out[...] = (preact * gating).astype(bf16)
    slope = gating * (1.0 + preact * (1.0 - gating))
    grad_pre = (cot[...].astype(f32) * slope).astype(bf16)
    grad_hidden = lax.dot_general(grad_pre, w, (((1,), (1,)), ((), ())), preferred_element_type=f32).astype(bf16)
    for r in range(N_REP):
        payload[r] = grad_hidden
    weight_part[...] = lax.dot_general(
        hidden, grad_pre, (((0,), (0,)), ((), ())), preferred_element_type=f32
    ).astype(bf16)


def on_device(node_features, tile_values, tile_row, tile_col, tile_count, weight, cotangent):
    sds = jax.ShapeDtypeStruct
    smem = pl.BlockSpec(memory_space=pltpu.SMEM)
    vmem = pl.BlockSpec(memory_space=pltpu.VMEM)
    params = pltpu.CompilerParams(vmem_limit_bytes=VMEM_LIMIT)
    acc_rows = sds((ROW_BLOCKS + 1, TILE, F), f32)
    hbm = pl.BlockSpec(memory_space=pltpu.HBM)
    tiles = pltpu.with_memory_space_constraint(tile_values[0, 0], pltpu.HBM)
    tile_room = [pltpu.VMEM((SLOTS, TILE, TILE), bf16), pltpu.SemaphoreType.DMA((SLOTS // UNROLL,))]
    my_core = lax.axis_index("core")
    my_xl = lax.axis_index("xl")

    def call(kernel, name, out_shape, *args, scratch=()):
        return pl.pallas_call(
            kernel,
            out_shape=out_shape,
            in_specs=[smem, hbm] + [vmem] * (len(args) - 2),
            out_specs=vmem,
            scratch_shapes=tile_room + list(scratch),
            compiler_params=params,
            cost_estimate=pl.CostEstimate(flops=1, transcendentals=0, bytes_accessed=1),
            name=name,
        )(*args)

    with jax.named_scope("slot_table"):
        table = slot_table(tile_row[0, 0], tile_col[0, 0], tile_count[0, 0], my_xl, my_core)
    with jax.named_scope("gather_features"):
        first = jnp.broadcast_to(node_features[None, :TILE], (N_Z, TILE, F))
        near0 = lax.all_to_all(first, "z", 0, 0, tiled=True)
        own = node_features[TILE:]
        other = xor_swap(own, "xl", 2, 1)
        pair = jnp.broadcast_to(jnp.stack([own, other])[None], (N_Z, 2, TILE, F))
        near0, pair, table = lax.optimization_barrier((near0, pair, table))
        near_pair = lax.all_to_all(pair, "z", 0, 0, tiled=True).reshape(2 * N_Z, TILE, F)
        near1 = xor_swap(near0, "xl", 2, 1)
        far0 = xor_swap(near0, "core", 2, 1)
        far1 = xor_swap(near1, "core", 2, 1)
    with jax.named_scope("tile_products"):
        acc = call(forward_first_kernel, "tile_products_first", acc_rows, table, tiles, near0, near1, far0, far1)
        near_pair, acc = lax.optimization_barrier((near_pair, acc))
        far_pair = xor_swap(near_pair, "core", 2, 1)
        acc = call(forward_second_kernel, "tile_products_second", acc_rows, table, tiles, near_pair, acc)
        partial = call(
            forward_last_kernel,
            "tile_products_last",
            sds((N_REP, XR, F), bf16),
            table,
            tiles,
            far_pair,
            acc,
            scratch=[pltpu.VMEM((ROW_BLOCKS + 1, TILE, F), f32)],
        )
    with jax.named_scope("sum_partials"):
        parts = lax.all_to_all(partial, REP, 0, 0, tiled=True)
    with jax.named_scope("dense"):
        layer_out, payload, weight_part = pl.pallas_call(
            dense_kernel,
            out_shape=(sds((XR, F), bf16), sds((N_REP, XR, F), bf16), sds((F, F), bf16)),
            in_specs=[vmem] * 3,
            out_specs=[vmem] * 3,
            compiler_params=params,
            name="dense",
        )(parts, weight, cotangent[0, 0])
    with jax.named_scope("share_gradients"):
        grads = lax.all_to_all(payload, REP, 0, 0, tiled=True)
    with jax.named_scope("weight_z"):
        w = weight_part
        for bit in (1, 2, 4):
            w = add_swapped(w, "z", N_Z, bit)
        grads, w = lax.optimization_barrier((grads, w))

    def backward(ranges, name, *holders):
        n = len(ranges)
        return pl.pallas_call(
            lambda *refs: backward_kernel(ranges, *refs),
            out_shape=[sds((2 * N_Z, TILE, F), bf16)] * n,
            in_specs=[smem, hbm] + [vmem] * (1 + len(holders)),
            out_specs=[vmem] * n,
            scratch_shapes=[
                pltpu.VMEM((n, SLOTS, TILE, TILE), bf16),
                pltpu.SemaphoreType.DMA((n, SLOTS // UNROLL)),
                pltpu.VMEM((2 * N_Z + 1, TILE, F), f32),
            ],
            compiler_params=pltpu.CompilerParams(vmem_limit_bytes=VMEM_LIMIT),
            cost_estimate=pl.CostEstimate(flops=1, transcendentals=0, bytes_accessed=1),
            name=name,
        )(table, tiles, grads, *holders)

    with jax.named_scope("back_second"):
        far_second, far_first = backward(((5, 6), (2, 4)), "back_far")
        got = xor_swap(far_second, "core", 2, 1)
        first_got = xor_swap(far_first, "core", 2, 1)
        (near_back,) = backward(((4, 5),), "back_second_near")
        pair = (near_back.astype(f32) + got.astype(f32)).astype(bf16)
        pair_small, w = hold(pair, w)
        pair_got = lax.all_to_all(pair.reshape(N_Z, 2, TILE, F), "z", 0, 0, tiled=True)
    with jax.named_scope("back_first"):
        got = first_got
        (near_back,) = backward(((0, 2),), "back_first_near", pair_small)
        away = (near_back[N_Z:].astype(f32) + got[N_Z:].astype(f32)).astype(bf16)
        back = xor_swap(away, "xl", 2, 1)
        w1, w2, w3 = (xor_swap(w, "y", N_Y, bit).astype(f32) for bit in (1, 2, 3))
        w = ((w.astype(f32) + w1) + (w2 + w3)).astype(bf16)
        home = (near_back[:N_Z].astype(f32) + got[:N_Z].astype(f32) + back.astype(f32)).astype(bf16)
        home, w, pair_got = lax.optimization_barrier((home, w, pair_got))
        home_got = lax.all_to_all(home, "z", 0, 0, tiled=True)
    with jax.named_scope("grad_features"):
        pair_sum = jnp.sum(pair_got.astype(f32), axis=0)
        back = xor_swap(pair_sum[1].astype(bf16), "xl", 2, 1)
        second_sum = (pair_sum[0] + back.astype(f32)).astype(bf16)
        first_sum = jnp.sum(home_got.astype(f32), axis=0).astype(bf16)
        grad_features = jnp.concatenate([first_sum, second_sum], axis=0)
    with jax.named_scope("weight_rest"):
        home_small, w = hold(pair_got, w)
        w = add_swapped(w, "xl", 2, 1)
        w = add_swapped(w, "xh", 2, 1)
        grad_weight = pl.pallas_call(
            final_weight_kernel,
            out_shape=sds((F, F), f32),
            in_specs=[vmem] * 3,
            out_specs=vmem,
            compiler_params=params,
            name="final_weight",
        )(w, xor_swap(w, "core", 2, 1), home_small)
    return layer_out.reshape(1, 1, XR, F), grad_weight, grad_features


def solution(mesh):
    fine = Mesh(np.asarray(mesh.devices).reshape(N_Y, 2, N_Z, 2, 2), REP + BLK)
    placed = (
        P(REP + BLK, None),
        P(REP, BLK, None, None, None),
        P(REP, BLK, None),
        P(REP, BLK, None),
        P(REP, BLK),
        P(),
        P(BLK, REP, None, None),
    )
    return jax.shard_map(
        on_device,
        mesh=fine,
        in_specs=placed,
        out_specs=(P(BLK, REP, None, None), P(), P(REP + BLK, None)),
        check_vma=False,
    )
```

```python
import jax
import jax.numpy as jnp
import numpy as np
from jax import lax
from jax.experimental import pallas as pl
from jax.experimental.pallas import tpu as pltpu
from jax.sharding import Mesh
from jax.sharding import PartitionSpec as P

REP = ("y", "xh")
BLK = ("z", "xl", "core")
N_Z = 8
N_Y = 4
TILE = 128
F = 256
XR = 256
N_REP = 8
SLOTS = 128
ROW_BLOCKS = 16
UNROLL = 8
CLASSES = 6

f32 = jnp.float32
bf16 = jnp.bfloat16
VMEM_LIMIT = 16 << 20


def xor_swap(x, axis, n, bit):
    return lax.ppermute(x, axis, [(i, i ^ bit) for i in range(n)])


def add_swapped(x, axis, n, bit):
    return (x.astype(f32) + xor_swap(x, axis, n, bit).astype(f32)).astype(bf16)


def hold(operand, value):
    return lax.optimization_barrier((operand.reshape(-1, F)[:16], value))


def slot_table(rows, cols, count, my_xl, my_core):
    owner = cols >> 1
    z = owner >> 2
    dx = ((owner >> 1) & 1) ^ my_xl
    dc = (owner & 1) ^ my_core
    second = (cols & 1) == 1
    position = jnp.arange(SLOTS, dtype=jnp.int32)
    kind = jnp.where(position < count, jnp.where(second, 4 + dc, 2 * dc + dx), CLASSES)
    place = jnp.where(second, z * 2 + dx, dx * N_Z + z)
    packed = rows | (place << 8) | (position << 16)
    key = kind * SLOTS + position
    rank = jnp.sum((key[None, :] < key[:, None]).astype(jnp.int32), axis=1)
    ordered = jnp.sum(jnp.where(rank[None, :] == position[:, None], packed[None, :], 0), axis=1)
    starts = jnp.sum((kind[None, :] < position[:, None]).astype(jnp.int32), axis=1)
    return jnp.concatenate([jnp.stack([ordered, starts]), jnp.zeros((2, SLOTS), jnp.int32)], axis=1)


def slot_range(table, first, last):
    begin = table[1, first]
    return begin, (table[1, last] - begin + UNROLL - 1) // UNROLL


def start_tiles(table, first, last, tiles_hbm, tiles, sems):
    begin, rounds = slot_range(table, first, last)

    def start(i, carry):
        for u in range(UNROLL):
            at = i * UNROLL + u
            pltpu.make_async_copy(tiles_hbm.at[table[0, begin + at] >> 16], tiles.at[at], sems.at[i]).start()
        return carry

    lax.fori_loop(0, rounds, start, 0)


def slot_loop(table, first, last, tiles_hbm, tiles, sems, one_slot):
    begin, rounds = slot_range(table, first, last)
    end = table[1, last]

    def step(i, carry):
        pltpu.make_async_copy(
            tiles_hbm.at[pl.ds(0, UNROLL)], tiles.at[pl.ds(i * UNROLL, UNROLL)], sems.at[i]
        ).wait()
        for u in range(UNROLL):
            t = begin + i * UNROLL + u
            packed = table[0, t]
            one_slot(t < end, packed & 255, (packed >> 8) & 255, tiles[i * UNROLL + u])
        return carry

    lax.fori_loop(0, rounds, step, 0)


def add_products(table, first, feats, mask, acc, room):
    def one_slot(live, row, place, tile):
        target = jnp.where(live, row, ROW_BLOCKS)
        acc[target] += jnp.dot(tile, feats[place & mask], preferred_element_type=f32)

    slot_loop(table, first, first + 1, *room, one_slot)


def forward_first_kernel(table, tiles_hbm, near0, near1, far0, far1, acc, tiles, sems):
    begin = table[1, 0]
    start_tiles(table, 0, 4, tiles_hbm, tiles, sems)
    acc[...] = jnp.zeros_like(acc)
    _, rounds = slot_range(table, 0, 4)

    def wait(i, carry):
        pltpu.make_async_copy(
            tiles_hbm.at[pl.ds(0, UNROLL)], tiles.at[pl.ds(i * UNROLL, UNROLL)], sems.at[i]
        ).wait()
        return carry

    lax.fori_loop(0, rounds, wait, 0)
    for k, feats in enumerate((near0, near1, far0, far1)):
        first, steps = slot_range(table, k, k + 1)
        end = table[1, k + 1]

        def step(i, carry):
            for u in range(UNROLL):
                t = first + i * UNROLL + u
                packed = table[0, t]
                target = jnp.where(t < end, packed & 255, ROW_BLOCKS)
                at = jnp.minimum(t - begin, SLOTS - 1)
                acc[target] += jnp.dot(
                    tiles[at], feats[(packed >> 8) & (N_Z - 1)], preferred_element_type=f32
                )
            return carry

        lax.fori_loop(0, steps, step, 0)


def forward_second_kernel(table, tiles_hbm, feats, before, acc, tiles, sems):
    start_tiles(table, 4, 5, tiles_hbm, tiles, sems)
    acc[...] = before[...]
    add_products(table, 4, feats, 2 * N_Z - 1, acc, (tiles_hbm, tiles, sems))


def forward_last_kernel(table, tiles_hbm, feats, before, out, tiles, sems, acc):
    start_tiles(table, 5, 6, tiles_hbm, tiles, sems)
    acc[...] = before[...]
    add_products(table, 5, feats, 2 * N_Z - 1, acc, (tiles_hbm, tiles, sems))
    for r in range(N_REP):
        for h in range(2):
            out[r, pl.ds(h * TILE, TILE), :] = acc[2 * r + h].astype(bf16)


def backward_kernel(ranges, table, tiles_hbm, grads, *rest):
    tiles, sems, acc = rest[-3:]
    outs = rest[-3 - len(ranges) : -3]
    for n, (first, last) in enumerate(ranges):
        start_tiles(table, first, last, tiles_hbm, tiles.at[n], sems.at[n])
    for n, ((first, last), out) in enumerate(zip(ranges, outs)):
        acc[...] = jnp.zeros_like(acc)

        def one_slot(live, row, place, tile):
            target = jnp.where(live, place, 2 * N_Z)
            g = grads[row >> 1, pl.ds(pl.multiple_of((row & 1) * TILE, TILE), TILE), :]
            acc[target] += lax.dot_general(tile, g, (((0,), (0,)), ((), ())), preferred_element_type=f32)

        slot_loop(table, first, last, tiles_hbm, tiles.at[n], sems.at[n], one_slot)
        for k in range(2 * N_Z):
            out[k] = acc[k].astype(bf16)


def half_of(core, which):
    return pl.ds(pl.multiple_of((core[0] if which == 0 else 1 - core[0]) * TILE, TILE), TILE)


def final_weight_kernel(core, mine, other, holder, out):
    out[half_of(core, 0), :] = mine[...].astype(f32)
    out[half_of(core, 1), :] = other[...].astype(f32)


def pair_copies_kernel(own, other, out):
    for z in range(N_Z):
        out[z, 0] = own[...]
        out[z, 1] = other[...]


def dense_kernel(core, parts, weight, cot, layer_out, payload, keep, give, terms):
    total = parts[0].astype(f32)
    for r in range(1, N_REP):
        total += parts[r].astype(f32)
    hidden = total.astype(bf16)
    w = weight[...]
    preact = jnp.dot(hidden, w, preferred_element_type=f32)
    gating = jax.nn.sigmoid(preact)
    layer_out[...] = (preact * gating).astype(bf16)
    slope = gating * (1.0 + preact * (1.0 - gating))
    grad_pre = (cot[...].astype(f32) * slope).astype(bf16)
    grad_hidden = lax.dot_general(grad_pre, w, (((1,), (1,)), ((), ())), preferred_element_type=f32).astype(bf16)
    for r in range(N_REP):
        payload[r] = grad_hidden
    terms[...] = lax.dot_general(hidden, grad_pre, (((0,), (0,)), ((), ())), preferred_element_type=f32)
    keep[...] = terms[half_of(core, 0), :].astype(bf16)
    give[...] = terms[half_of(core, 1), :].astype(bf16)


def on_device(node_features, tile_values, tile_row, tile_col, tile_count, weight, cotangent):
    sds = jax.ShapeDtypeStruct
    smem = pl.BlockSpec(memory_space=pltpu.SMEM)
    vmem = pl.BlockSpec(memory_space=pltpu.VMEM)
    params = pltpu.CompilerParams(vmem_limit_bytes=VMEM_LIMIT)
    acc_rows = sds((ROW_BLOCKS + 1, TILE, F), f32)
    hbm = pl.BlockSpec(memory_space=pltpu.HBM)
    tiles = pltpu.with_memory_space_constraint(tile_values[0, 0], pltpu.HBM)
    tile_room = [pltpu.VMEM((SLOTS, TILE, TILE), bf16), pltpu.SemaphoreType.DMA((SLOTS // UNROLL,))]
    my_core = lax.axis_index("core")
    my_xl = lax.axis_index("xl")

    def call(kernel, name, out_shape, *args, scratch=()):
        return pl.pallas_call(
            kernel,
            out_shape=out_shape,
            in_specs=[smem, hbm] + [vmem] * (len(args) - 2),
            out_specs=vmem,
            scratch_shapes=tile_room + list(scratch),
            compiler_params=params,
            cost_estimate=pl.CostEstimate(flops=1, transcendentals=0, bytes_accessed=1),
            name=name,
        )(*args)

    with jax.named_scope("slot_table"):
        table = slot_table(tile_row[0, 0], tile_col[0, 0], tile_count[0, 0], my_xl, my_core)
    with jax.named_scope("gather_features"):
        first = jnp.broadcast_to(node_features[None, :TILE], (N_Z, TILE, F))
        near0 = lax.all_to_all(first, "z", 0, 0, tiled=True)
        own = node_features[TILE:]
        other = xor_swap(own, "xl", 2, 1)
        pair = pl.pallas_call(
            pair_copies_kernel,
            out_shape=sds((N_Z, 2, TILE, F), bf16),
            in_specs=[vmem] * 2,
            out_specs=vmem,
            compiler_params=params,
            name="pair_copies",
        )(own, other)
        near0, pair, table = lax.optimization_barrier((near0, pair, table))
        near_pair = lax.all_to_all(pair, "z", 0, 0, tiled=True).reshape(2 * N_Z, TILE, F)
        near1 = xor_swap(near0, "xl", 2, 1)
        far0 = xor_swap(near0, "core", 2, 1)
        far1 = xor_swap(near1, "core", 2, 1)
    with jax.named_scope("tile_products"):
        acc = call(forward_first_kernel, "tile_products_first", acc_rows, table, tiles, near0, near1, far0, far1)
        near_pair, acc = lax.optimization_barrier((near_pair, acc))
        far_pair = xor_swap(near_pair, "core", 2, 1)
        acc = call(forward_second_kernel, "tile_products_second", acc_rows, table, tiles, near_pair, acc)
        partial = call(
            forward_last_kernel,
            "tile_products_last",
            sds((N_REP, XR, F), bf16),
            table,
            tiles,
            far_pair,
            acc,
            scratch=[pltpu.VMEM((ROW_BLOCKS + 1, TILE, F), f32)],
        )
    with jax.named_scope("sum_partials"):
        parts = lax.all_to_all(partial, REP, 0, 0, tiled=True)
    with jax.named_scope("dense"):
        core = my_core.astype(jnp.int32).reshape(1)
        layer_out, payload, keep, give = pl.pallas_call(
            dense_kernel,
            out_shape=(
                sds((XR, F), bf16),
                sds((N_REP, XR, F), bf16),
                sds((TILE, F), bf16),
                sds((TILE, F), bf16),
            ),
            in_specs=[smem] + [vmem] * 3,
            out_specs=[vmem] * 4,
            scratch_shapes=[pltpu.VMEM((F, F), f32)],
            compiler_params=params,
            name="dense",
        )(core, parts, weight, cotangent[0, 0])
    with jax.named_scope("share_gradients"):
        grads = lax.all_to_all(payload, REP, 0, 0, tiled=True)
    with jax.named_scope("weight_z"):
        ring = [(2 * z + c, 2 * (z ^ 1) + (c ^ 1)) for z in range(N_Z) for c in range(2)]
        near_give = xor_swap(give, "core", 2, 1).astype(f32)
        far_give = lax.ppermute(give, ("z", "core"), ring).astype(f32)
        far_keep = xor_swap(keep, "z", N_Z, 1).astype(f32)
        w = ((keep.astype(f32) + near_give) + (far_keep + far_give)).astype(bf16)
        for bit in (2, 4):
            w = add_swapped(w, "z", N_Z, bit)
        grads, w = lax.optimization_barrier((grads, w))

    def backward(ranges, name, *holders):
        n = len(ranges)
        return pl.pallas_call(
            lambda *refs: backward_kernel(ranges, *refs),
            out_shape=[sds((2 * N_Z, TILE, F), bf16)] * n,
            in_specs=[smem, hbm] + [vmem] * (1 + len(holders)),
            out_specs=[vmem] * n,
            scratch_shapes=[
                pltpu.VMEM((n, SLOTS, TILE, TILE), bf16),
                pltpu.SemaphoreType.DMA((n, SLOTS // UNROLL)),
                pltpu.VMEM((2 * N_Z + 1, TILE, F), f32),
            ],
            compiler_params=pltpu.CompilerParams(vmem_limit_bytes=VMEM_LIMIT),
            cost_estimate=pl.CostEstimate(flops=1, transcendentals=0, bytes_accessed=1),
            name=name,
        )(table, tiles, grads, *holders)

    with jax.named_scope("back_second"):
        far_second, far_first = backward(((5, 6), (2, 4)), "back_far")
        got = xor_swap(far_second, "core", 2, 1)
        first_got = xor_swap(far_first, "core", 2, 1)
        (near_back,) = backward(((4, 5),), "back_second_near")
        pair = (near_back.astype(f32) + got.astype(f32)).astype(bf16)
        pair_small, w = hold(pair, w)
        pair_got = lax.all_to_all(pair.reshape(N_Z, 2, TILE, F), "z", 0, 0, tiled=True)
    with jax.named_scope("back_first"):
        got = first_got
        (near_back,) = backward(((0, 2),), "back_first_near", pair_small)
        away = (near_back[N_Z:].astype(f32) + got[N_Z:].astype(f32)).astype(bf16)
        back = xor_swap(away, "xl", 2, 1)
        w1, w2, w3 = (xor_swap(w, "y", N_Y, bit).astype(f32) for bit in (1, 2, 3))
        w = ((w.astype(f32) + w1) + (w2 + w3)).astype(bf16)
        home = (near_back[:N_Z].astype(f32) + got[:N_Z].astype(f32) + back.astype(f32)).astype(bf16)
        home, w, pair_got = lax.optimization_barrier((home, w, pair_got))
        home_got = lax.all_to_all(home, "z", 0, 0, tiled=True)
    with jax.named_scope("grad_features"):
        pair_sum, w = lax.optimization_barrier((jnp.sum(pair_got.astype(f32), axis=0), w))
        back = xor_swap(pair_sum[1].astype(bf16), "xl", 2, 1)
        second_sum = (pair_sum[0] + back.astype(f32)).astype(bf16)
        first_sum = jnp.sum(home_got.astype(f32), axis=0).astype(bf16)
        grad_features = jnp.concatenate([first_sum, second_sum], axis=0)
    with jax.named_scope("weight_rest"):
        def from_x(dh, dl):
            ring = [(2 * h + l, 2 * (h ^ dh) + (l ^ dl)) for h in range(2) for l in range(2)]
            return lax.ppermute(w, ("xh", "xl"), ring).astype(f32)

        w = ((w.astype(f32) + from_x(0, 1)) + (from_x(1, 0) + from_x(1, 1))).astype(bf16)
        grad_weight = pl.pallas_call(
            final_weight_kernel,
            out_shape=sds((F, F), f32),
            in_specs=[smem] + [vmem] * 3,
            out_specs=vmem,
            compiler_params=params,
            name="final_weight",
        )(core, w, xor_swap(w, "core", 2, 1), pair_sum)
    return layer_out.reshape(1, 1, XR, F), grad_weight, grad_features


def solution(mesh):
    fine = Mesh(np.asarray(mesh.devices).reshape(N_Y, 2, N_Z, 2, 2), REP + BLK)
    placed = (
        P(REP + BLK, None),
        P(REP, BLK, None, None, None),
        P(REP, BLK, None),
        P(REP, BLK, None),
        P(REP, BLK),
        P(),
        P(BLK, REP, None, None),
    )
    return jax.shard_map(
        on_device,
        mesh=fine,
        in_specs=placed,
        out_specs=(P(BLK, REP, None, None), P(), P(REP + BLK, None)),
        check_vma=False,
    )
```

```python
import jax
import jax.numpy as jnp
import numpy as np
from jax import lax
from jax.experimental import pallas as pl
from jax.experimental.pallas import tpu as pltpu
from jax.sharding import Mesh
from jax.sharding import PartitionSpec as P

REP = ("y", "xh")
BLK = ("z", "xl", "core")
N_Z = 8
N_Y = 4
TILE = 128
F = 256
XR = 256
N_REP = 8
SLOTS = 128
ROW_BLOCKS = 16
UNROLL = 8
HALF = XR // 2
CLASSES = 2
CHUNKS = 2 * N_Z

f32 = jnp.float32
bf16 = jnp.bfloat16
VMEM_LIMIT = 16 << 20


def xor_swap(x, axis, n, bit):
    return lax.ppermute(x, axis, [(i, i ^ bit) for i in range(n)])


def add_swapped(x, axis, n, bit):
    return (x.astype(f32) + xor_swap(x, axis, n, bit).astype(f32)).astype(bf16)


def shift(x, step):
    return lax.ppermute(x, "z", [(i, (i + step) % N_Z) for i in range(N_Z)])


def slot_table(rows, cols, count, my_z, my_xl, my_core):
    owner = cols >> 1
    dz = ((owner >> 2) - my_z) & (N_Z - 1)
    dx = ((owner >> 1) & 1) ^ my_xl
    dc = (owner & 1) ^ my_core
    position = jnp.arange(SLOTS, dtype=jnp.int32)
    kind = jnp.where(position < count, dc, CLASSES)
    place = ((dx * N_Z + dz) << 1) | (cols & 1)
    packed = rows | (place << 8) | (position << 16)
    key = kind * SLOTS + position
    rank = jnp.sum((key[None, :] < key[:, None]).astype(jnp.int32), axis=1)
    ordered = jnp.sum(jnp.where(rank[None, :] == position[:, None], packed[None, :], 0), axis=1)
    starts = jnp.sum((kind[None, :] < position[:, None]).astype(jnp.int32), axis=1)
    return jnp.concatenate([jnp.stack([ordered, starts]), jnp.zeros((2, SLOTS), jnp.int32)], axis=1)


def slot_range(table, first, last):
    begin = table[1, first]
    return begin, (table[1, last] - begin + UNROLL - 1) // UNROLL


def start_tiles(table, first, last, tiles_hbm, tiles, sems):
    begin, rounds = slot_range(table, first, last)

    def start(i, carry):
        for u in range(UNROLL):
            at = i * UNROLL + u
            pltpu.make_async_copy(tiles_hbm.at[table[0, begin + at] >> 16], tiles.at[at], sems.at[i]).start()
        return carry

    lax.fori_loop(0, rounds, start, 0)


def slot_loop(table, first, last, tiles_hbm, tiles, sems, one_slot):
    begin, rounds = slot_range(table, first, last)
    end = table[1, last]

    def step(i, carry):
        pltpu.make_async_copy(
            tiles_hbm.at[pl.ds(0, UNROLL)], tiles.at[pl.ds(i * UNROLL, UNROLL)], sems.at[i]
        ).wait()
        for u in range(UNROLL):
            t = begin + i * UNROLL + u
            packed = table[0, t]
            one_slot(t < end, packed & 255, (packed >> 8) & 255, tiles[i * UNROLL + u])
        return carry

    lax.fori_loop(0, rounds, step, 0)


def tile_of(ref, which):
    return ref[which >> 1, pl.ds(pl.multiple_of((which & 1) * TILE, TILE), TILE), :]


def assemble_kernel(*refs):
    out, sems = refs[-2:]
    copies = []
    for n, src in enumerate(refs[:-2]):
        dx, k = divmod(n, N_Z + 1)
        if k < 4:
            dst = out.at[dx * N_Z + k]
        elif k < 6:
            dst = out.at[dx * N_Z + 4, pl.ds((k - 4) * HALF, HALF)]
        else:
            dst = out.at[dx * N_Z + k - 1]
        copies.append(pltpu.make_async_copy(src, dst, sems.at[n]))
    for c in copies:
        c.start()
    for c in copies:
        c.wait()


def add_products(table, first, feats, acc, room):
    def one_slot(live, row, place, tile):
        target = jnp.where(live, row, ROW_BLOCKS)
        acc[target] += jnp.dot(tile, tile_of(feats, place), preferred_element_type=f32)

    slot_loop(table, first, first + 1, *room, one_slot)


def forward_near_kernel(table, tiles_hbm, feats, acc, tiles, sems):
    start_tiles(table, 0, 1, tiles_hbm, tiles, sems)
    acc[...] = jnp.zeros_like(acc)
    add_products(table, 0, feats, acc, (tiles_hbm, tiles, sems))


def forward_far_kernel(table, tiles_hbm, feats, before, out, tiles, sems, acc):
    start_tiles(table, 1, 2, tiles_hbm, tiles, sems)
    acc[...] = before[...]
    add_products(table, 1, feats, acc, (tiles_hbm, tiles, sems))
    for r in range(N_REP):
        for h in range(2):
            out[r, pl.ds(h * TILE, TILE), :] = acc[2 * r + h].astype(bf16)


def backward_kernel(first, table, tiles_hbm, grads, out, tiles, sems, acc):
    start_tiles(table, first, first + 1, tiles_hbm, tiles, sems)
    acc[...] = jnp.zeros_like(acc)

    def one_slot(live, row, place, tile):
        target = jnp.where(live, place, 2 * CHUNKS)
        acc[target] += lax.dot_general(
            tile, tile_of(grads, row), (((0,), (0,)), ((), ())), preferred_element_type=f32
        )

    slot_loop(table, first, first + 1, tiles_hbm, tiles, sems, one_slot)
    for k in range(CHUNKS):
        for h in range(2):
            out[k, pl.ds(h * TILE, TILE), :] = acc[2 * k + h].astype(bf16)


def half_of(core, which):
    return pl.ds(pl.multiple_of((core[0] if which == 0 else 1 - core[0]) * TILE, TILE), TILE)


def final_weight_kernel(core, mine, other, out):
    out[half_of(core, 0), :] = mine[...].astype(f32)
    out[half_of(core, 1), :] = other[...].astype(f32)


def dense_kernel(core, parts, weight, cot, layer_out, payload, keep, give, terms):
    total = parts[0].astype(f32)
    for r in range(1, N_REP):
        total += parts[r].astype(f32)
    hidden = total.astype(bf16)
    w = weight[...]
    preact = jnp.dot(hidden, w, preferred_element_type=f32)
    gating = jax.nn.sigmoid(preact)
    layer_out[...] = (preact * gating).astype(bf16)
    slope = gating * (1.0 + preact * (1.0 - gating))
    grad_pre = (cot[...].astype(f32) * slope).astype(bf16)
    grad_hidden = lax.dot_general(grad_pre, w, (((1,), (1,)), ((), ())), preferred_element_type=f32).astype(bf16)
    for r in range(N_REP):
        payload[r] = grad_hidden
    terms[...] = lax.dot_general(hidden, grad_pre, (((0,), (0,)), ((), ())), preferred_element_type=f32)
    keep[...] = terms[half_of(core, 0), :].astype(bf16)
    give[...] = terms[half_of(core, 1), :].astype(bf16)


def on_device(node_features, tile_values, tile_row, tile_col, tile_count, weight, cotangent):
    sds = jax.ShapeDtypeStruct
    smem = pl.BlockSpec(memory_space=pltpu.SMEM)
    vmem = pl.BlockSpec(memory_space=pltpu.VMEM)
    params = pltpu.CompilerParams(vmem_limit_bytes=VMEM_LIMIT)
    acc_rows = sds((ROW_BLOCKS + 1, TILE, F), f32)
    hbm = pl.BlockSpec(memory_space=pltpu.HBM)
    tiles = pltpu.with_memory_space_constraint(tile_values[0, 0], pltpu.HBM)
    tile_room = [pltpu.VMEM((SLOTS, TILE, TILE), bf16), pltpu.SemaphoreType.DMA((SLOTS // UNROLL,))]
    my_core = lax.axis_index("core")
    my_xl = lax.axis_index("xl")

    def call(kernel, name, out_shape, *args, scratch=()):
        return pl.pallas_call(
            kernel,
            out_shape=out_shape,
            in_specs=[smem, hbm] + [vmem] * (len(args) - 2),
            out_specs=vmem,
            scratch_shapes=tile_room + list(scratch),
            compiler_params=params,
            cost_estimate=pl.CostEstimate(flops=1, transcendentals=0, bytes_accessed=1),
            name=name,
        )(*args)

    with jax.named_scope("gather_features"):
        up = down = node_features
        near = {0: node_features}
        for k in (1, 2, 3):
            up, down = shift(up, 1), shift(down, -1)
            near[N_Z - k], near[k] = up, down
        halves = [shift(up[:HALF], 1), shift(down[HALF:], -1)]
        order = [near[0], near[1], near[2], near[3]] + halves + [near[5], near[6], near[7]]
        chunks = order + [xor_swap(c, "xl", 2, 1) for c in order]
    with jax.named_scope("slot_table"):
        table = slot_table(
            tile_row[0, 0], tile_col[0, 0], tile_count[0, 0], lax.axis_index("z"), my_xl, my_core
        )
    with jax.named_scope("tile_products"):
        near_feats = pl.pallas_call(
            assemble_kernel,
            out_shape=sds((CHUNKS, XR, F), bf16),
            in_specs=[pl.BlockSpec(memory_space=pl.ANY)] * len(chunks),
            out_specs=vmem,
            scratch_shapes=[pltpu.SemaphoreType.DMA((len(chunks),))],
            compiler_params=params,
            name="assemble",
        )(*chunks)
        far_feats = xor_swap(near_feats, "core", 2, 1)
        acc = call(forward_near_kernel, "tile_products_near", acc_rows, table, tiles, near_feats)
        partial = call(
            forward_far_kernel,
            "tile_products_far",
            sds((N_REP, XR, F), bf16),
            table,
            tiles,
            far_feats,
            acc,
            scratch=[pltpu.VMEM((ROW_BLOCKS + 1, TILE, F), f32)],
        )
    with jax.named_scope("sum_partials"):
        parts = lax.all_to_all(partial, REP, 0, 0, tiled=True)
    with jax.named_scope("dense"):
        core = my_core.astype(jnp.int32).reshape(1)
        layer_out, payload, keep, give = pl.pallas_call(
            dense_kernel,
            out_shape=(
                sds((XR, F), bf16),
                sds((N_REP, XR, F), bf16),
                sds((TILE, F), bf16),
                sds((TILE, F), bf16),
            ),
            in_specs=[smem] + [vmem] * 3,
            out_specs=[vmem] * 4,
            scratch_shapes=[pltpu.VMEM((F, F), f32)],
            compiler_params=params,
            name="dense",
        )(core, parts, weight, cotangent[0, 0])
    with jax.named_scope("share_gradients"):
        grads = lax.all_to_all(payload, REP, 0, 0, tiled=True)
    with jax.named_scope("weight_z"):
        ring = [(2 * z + c, 2 * (z ^ 1) + (c ^ 1)) for z in range(N_Z) for c in range(2)]
        near_give = xor_swap(give, "core", 2, 1).astype(f32)
        far_give = lax.ppermute(give, ("z", "core"), ring).astype(f32)
        far_keep = xor_swap(keep, "z", N_Z, 1).astype(f32)
        w = ((keep.astype(f32) + near_give) + (far_keep + far_give)).astype(bf16)
        w = add_swapped(w, "z", N_Z, 2)
        grads, w = lax.optimization_barrier((grads, w))
        w = add_swapped(w, "z", N_Z, 4)

    def backward(first, name):
        return call(
            lambda *refs: backward_kernel(first, *refs),
            name,
            sds((CHUNKS, XR, F), bf16),
            table,
            tiles,
            grads,
            scratch=[pltpu.VMEM((2 * CHUNKS + 1, TILE, F), f32)],
        )

    def total(*terms):
        return sum(t.astype(f32) for t in terms).astype(bf16)

    with jax.named_scope("tile_products_back"):
        far_back = backward(1, "back_far")
        got = xor_swap(far_back, "core", 2, 1)
        back = total(backward(0, "back_near"), got)
        back, w = lax.optimization_barrier((back, w))
    with jax.named_scope("scatter_gradients"):
        away = {d: xor_swap(back[N_Z + d], "xl", 2, 1) for d in (4, 3, 5, 2, 6, 1, 7, 0)}
        far = total(back[4], away[4])
        up, down = shift(far[:HALF], 1), shift(far[HALF:], -1)
        none = jnp.zeros_like(up)
        up, down = jnp.concatenate([up, none], axis=0), jnp.concatenate([none, down], axis=0)
        for d in (3, 2, 1):
            up = shift(total(back[d], away[d], up), 1)
            down = shift(total(back[N_Z - d], away[N_Z - d], down), -1)
        grad_features = total(back[0], away[0], up, down)
    with jax.named_scope("weight_rest"):
        for axis, n, bit in (("y", N_Y, 1), ("y", N_Y, 2), ("xl", 2, 1), ("xh", 2, 1)):
            w = add_swapped(w, axis, n, bit)
        grad_weight = pl.pallas_call(
            final_weight_kernel,
            out_shape=sds((F, F), f32),
            in_specs=[smem] + [vmem] * 2,
            out_specs=vmem,
            compiler_params=params,
            name="final_weight",
        )(core, w, xor_swap(w, "core", 2, 1))
    return layer_out.reshape(1, 1, XR, F), grad_weight, grad_features


def solution(mesh):
    fine = Mesh(np.asarray(mesh.devices).reshape(N_Y, 2, N_Z, 2, 2), REP + BLK)
    placed = (
        P(REP + BLK, None),
        P(REP, BLK, None, None, None),
        P(REP, BLK, None),
        P(REP, BLK, None),
        P(REP, BLK),
        P(),
        P(BLK, REP, None, None),
    )
    return jax.shard_map(
        on_device,
        mesh=fine,
        in_specs=placed,
        out_specs=(P(BLK, REP, None, None), P(), P(REP + BLK, None)),
        check_vma=False,
    )
```

```python
import jax
import jax.numpy as jnp
import numpy as np
from jax import lax
from jax.experimental import pallas as pl
from jax.experimental.pallas import tpu as pltpu
from jax.sharding import Mesh
from jax.sharding import PartitionSpec as P

REP = ("y", "xh")
BLK = ("z", "xl", "core")
N_Z = 8
N_Y = 4
TILE = 128
F = 256
XR = 256
N_REP = 8
SLOTS = 128
ROW_BLOCKS = 16
UNROLL = 8
HALF = XR // 2
CLASSES = 4
SPOT = {4: 0, 3: 1, 5: 2, 2: 3, 6: 4, 1: 5, 7: 6, 0: 7}

f32 = jnp.float32
bf16 = jnp.bfloat16
VMEM_LIMIT = 16 << 20


def xor_swap(x, axis, n, bit):
    return lax.ppermute(x, axis, [(i, i ^ bit) for i in range(n)])


def add_swapped(x, axis, n, bit):
    return (x.astype(f32) + xor_swap(x, axis, n, bit).astype(f32)).astype(bf16)


def shift(x, step):
    return lax.ppermute(x, "z", [(i, (i + step) % N_Z) for i in range(N_Z)])


def slot_table(rows, cols, count, my_z, my_xl, my_core):
    owner = cols >> 1
    dz = ((owner >> 2) - my_z) & (N_Z - 1)
    dx = ((owner >> 1) & 1) ^ my_xl
    dc = (owner & 1) ^ my_core
    position = jnp.arange(SLOTS, dtype=jnp.int32)
    kind = jnp.where(position < count, 2 * dx + dc, CLASSES)
    spot = jnp.maximum(2 * (4 - jnp.minimum(dz, N_Z - dz)) - 1 + (dz > 4).astype(jnp.int32), 0)
    place = (spot << 1) | (cols & 1)
    packed = rows | (place << 8) | (position << 16)
    key = kind * SLOTS + position
    rank = jnp.sum((key[None, :] < key[:, None]).astype(jnp.int32), axis=1)
    ordered = jnp.sum(jnp.where(rank[None, :] == position[:, None], packed[None, :], 0), axis=1)
    starts = jnp.sum((kind[None, :] < position[:, None]).astype(jnp.int32), axis=1)
    return jnp.concatenate([jnp.stack([ordered, starts]), jnp.zeros((2, SLOTS), jnp.int32)], axis=1)


def slot_range(table, first, last):
    begin = table[1, first]
    return begin, (table[1, last] - begin + UNROLL - 1) // UNROLL


def start_tiles(table, first, last, tiles_hbm, tiles, sems):
    begin, rounds = slot_range(table, first, last)

    def start(i, carry):
        for u in range(UNROLL):
            at = i * UNROLL + u
            pltpu.make_async_copy(tiles_hbm.at[table[0, begin + at] >> 16], tiles.at[at], sems.at[i]).start()
        return carry

    lax.fori_loop(0, rounds, start, 0)


def slot_loop(table, first, last, tiles_hbm, tiles, sems, one_slot):
    begin, rounds = slot_range(table, first, last)
    end = table[1, last]

    def step(i, carry):
        pltpu.make_async_copy(
            tiles_hbm.at[pl.ds(0, UNROLL)], tiles.at[pl.ds(i * UNROLL, UNROLL)], sems.at[i]
        ).wait()
        for u in range(UNROLL):
            t = begin + i * UNROLL + u
            packed = table[0, t]
            one_slot(t < end, packed & 255, (packed >> 8) & 255, tiles[i * UNROLL + u])
        return carry

    lax.fori_loop(0, rounds, step, 0)


def tile_of(ref, which):
    return ref[which >> 1, pl.ds(pl.multiple_of((which & 1) * TILE, TILE), TILE), :]


def blocks(n, one):
    def step(i, carry):
        one(i)
        return carry

    lax.fori_loop(0, n, step, 0)


def clear(acc):
    zero = jnp.zeros((TILE, F), f32)

    def one(i):
        acc[i] = zero

    blocks(acc.shape[0] - 1, one)


def carry_over(before, acc):
    def one(i):
        acc[i] = before[i]

    blocks(acc.shape[0] - 1, one)


def round_out(acc, out):
    def one(i):
        for h in range(2):
            out[i, pl.ds(h * TILE, TILE), :] = acc[2 * i + h].astype(bf16)

    blocks(out.shape[0], one)


def assemble_kernel(*refs):
    out, sems = refs[-2:]
    copies = []
    for k, src in enumerate(refs[:-2]):
        if k < 4:
            dst = out.at[SPOT[k]]
        elif k < 6:
            dst = out.at[SPOT[4], pl.ds((k - 4) * HALF, HALF)]
        else:
            dst = out.at[SPOT[k - 1]]
        copies.append(pltpu.make_async_copy(src, dst, sems.at[k]))
    for c in copies:
        c.start()
    for c in copies:
        c.wait()


def add_products(table, kind, feats, acc, room):
    def one_slot(live, row, place, tile):
        target = jnp.where(live, row, ROW_BLOCKS)
        acc[target] += jnp.dot(tile, tile_of(feats, place), preferred_element_type=f32)

    slot_loop(table, kind, kind + 1, *room, one_slot)


def forward_first_kernel(table, tiles_hbm, near, far, acc, tiles, sems):
    for k in range(2):
        start_tiles(table, k, k + 1, tiles_hbm, tiles.at[k], sems.at[k])
    clear(acc)
    for k, feats in enumerate((near, far)):
        add_products(table, k, feats, acc, (tiles_hbm, tiles.at[k], sems.at[k]))


def forward_near_kernel(table, tiles_hbm, feats, before, acc, tiles, sems):
    start_tiles(table, 2, 3, tiles_hbm, tiles.at[0], sems.at[0])
    carry_over(before, acc)
    add_products(table, 2, feats, acc, (tiles_hbm, tiles.at[0], sems.at[0]))


def forward_far_kernel(table, tiles_hbm, feats, before, out, tiles, sems, acc):
    start_tiles(table, 3, 4, tiles_hbm, tiles.at[0], sems.at[0])
    carry_over(before, acc)
    add_products(table, 3, feats, acc, (tiles_hbm, tiles.at[0], sems.at[0]))
    round_out(acc, out)


def backward_kernel(kind, table, tiles_hbm, grads, out, tiles, sems, acc):
    start_tiles(table, kind, kind + 1, tiles_hbm, tiles.at[0], sems.at[0])
    clear(acc)

    def one_slot(live, row, place, tile):
        target = jnp.where(live, place, 2 * N_Z)
        acc[target] += lax.dot_general(
            tile, tile_of(grads, row), (((0,), (0,)), ((), ())), preferred_element_type=f32
        )

    slot_loop(table, kind, kind + 1, tiles_hbm, tiles.at[0], sems.at[0], one_slot)
    round_out(acc, out)


def half_of(core, which):
    return pl.ds(pl.multiple_of((core[0] if which == 0 else 1 - core[0]) * TILE, TILE), TILE)


def final_weight_kernel(core, mine, other, out):
    out[half_of(core, 0), :] = mine[...].astype(f32)
    out[half_of(core, 1), :] = other[...].astype(f32)


def dense_kernel(core, parts, weight, cot, layer_out, payload, keep, give, terms):
    total = parts[0].astype(f32)
    for r in range(1, N_REP):
        total += parts[r].astype(f32)
    hidden = total.astype(bf16)
    w = weight[...]
    preact = jnp.dot(hidden, w, preferred_element_type=f32)
    gating = jax.nn.sigmoid(preact)
    layer_out[...] = (preact * gating).astype(bf16)
    slope = gating * (1.0 + preact * (1.0 - gating))
    grad_pre = (cot[...].astype(f32) * slope).astype(bf16)
    grad_hidden = lax.dot_general(grad_pre, w, (((1,), (1,)), ((), ())), preferred_element_type=f32).astype(bf16)
    for r in range(N_REP):
        payload[r] = grad_hidden
    terms[...] = lax.dot_general(hidden, grad_pre, (((0,), (0,)), ((), ())), preferred_element_type=f32)
    keep[...] = terms[half_of(core, 0), :].astype(bf16)
    give[...] = terms[half_of(core, 1), :].astype(bf16)


def on_device(node_features, tile_values, tile_row, tile_col, tile_count, weight, cotangent):
    sds = jax.ShapeDtypeStruct
    smem = pl.BlockSpec(memory_space=pltpu.SMEM)
    vmem = pl.BlockSpec(memory_space=pltpu.VMEM)
    params = pltpu.CompilerParams(vmem_limit_bytes=VMEM_LIMIT)
    acc_rows = sds((ROW_BLOCKS + 1, TILE, F), f32)
    hbm = pl.BlockSpec(memory_space=pltpu.HBM)
    tiles = pltpu.with_memory_space_constraint(tile_values[0, 0], pltpu.HBM)

    def tile_room(n):
        return [pltpu.VMEM((n, SLOTS, TILE, TILE), bf16), pltpu.SemaphoreType.DMA((n, SLOTS // UNROLL))]

    my_core = lax.axis_index("core")
    my_xl = lax.axis_index("xl")

    def call(kernel, name, out_shape, *args, scratch=(), rooms=1):
        return pl.pallas_call(
            kernel,
            out_shape=out_shape,
            in_specs=[smem, hbm] + [vmem] * (len(args) - 2),
            out_specs=vmem,
            scratch_shapes=tile_room(rooms) + list(scratch),
            compiler_params=params,
            cost_estimate=pl.CostEstimate(flops=1, transcendentals=0, bytes_accessed=1),
            name=name,
        )(*args)

    def across(x):
        return xor_swap(x, "xl", 2, 1)

    def assemble(chunks, name):
        return pl.pallas_call(
            assemble_kernel,
            out_shape=sds((N_Z, XR, F), bf16),
            in_specs=[pl.BlockSpec(memory_space=pl.ANY)] * len(chunks),
            out_specs=vmem,
            scratch_shapes=[pltpu.SemaphoreType.DMA((len(chunks),))],
            compiler_params=params,
            name=name,
        )(*chunks)

    with jax.named_scope("gather_features"):
        own = node_features
        up1, down1 = shift(own, 1), shift(own, -1)
        own_x = across(own)
        up2, down2 = shift(up1, 1), shift(down1, -1)
        up1_x, down1_x = across(up1), across(down1)
        up2, own_x = lax.optimization_barrier((up2, own_x))
        up3, down3 = shift(up2, 1), shift(down2, -1)
        up2_x, down2_x = across(up2), across(down2)
        up3, up1_x, down1_x = lax.optimization_barrier((up3, up1_x, down1_x))
        low, high = shift(up3[:HALF], 1), shift(down3[HALF:], -1)
        near0 = assemble((pltpu.with_memory_space_constraint(own, pltpu.HBM), down1, down2, down3, low, high, up3, up2, up1), "assemble_own")
        far0 = xor_swap(near0, "core", 2, 1)
        crossed = (own_x, down1_x, down2_x, across(down3), across(low), across(high), across(up3), up2_x, up1_x)
        near1 = assemble(crossed, "assemble_crossed")
        far1 = xor_swap(near1, "core", 2, 1)
    with jax.named_scope("slot_table"):
        table = slot_table(
            tile_row[0, 0], tile_col[0, 0], tile_count[0, 0], lax.axis_index("z"), my_xl, my_core
        )
    with jax.named_scope("tile_products"):
        acc = call(forward_first_kernel, "tile_products_first", acc_rows, table, tiles, near0, far0, rooms=2)
        acc = call(forward_near_kernel, "tile_products_near", acc_rows, table, tiles, near1, acc)
        partial = call(
            forward_far_kernel,
            "tile_products_far",
            sds((N_REP, XR, F), bf16),
            table,
            tiles,
            far1,
            acc,
            scratch=[pltpu.VMEM((ROW_BLOCKS + 1, TILE, F), f32)],
        )
    with jax.named_scope("sum_partials"):
        parts = lax.all_to_all(partial, REP, 0, 0, tiled=True)
    with jax.named_scope("dense"):
        core = my_core.astype(jnp.int32).reshape(1)
        layer_out, payload, keep, give = pl.pallas_call(
            dense_kernel,
            out_shape=(
                sds((XR, F), bf16),
                sds((N_REP, XR, F), bf16),
                sds((TILE, F), bf16),
                sds((TILE, F), bf16),
            ),
            in_specs=[smem] + [vmem] * 3,
            out_specs=[vmem] * 4,
            scratch_shapes=[pltpu.VMEM((F, F), f32)],
            compiler_params=params,
            name="dense",
        )(core, parts, weight, cotangent[0, 0])
    with jax.named_scope("share_gradients"):
        grads = lax.all_to_all(payload, REP, 0, 0, tiled=True)
    with jax.named_scope("weight_z"):
        ring = [(2 * z + c, 2 * (z ^ 1) + (c ^ 1)) for z in range(N_Z) for c in range(2)]
        near_give = xor_swap(give, "core", 2, 1).astype(f32)
        far_give = lax.ppermute(give, ("z", "core"), ring).astype(f32)
        far_keep = xor_swap(keep, "z", N_Z, 1).astype(f32)
        w = ((keep.astype(f32) + near_give) + (far_keep + far_give)).astype(bf16)
        w = add_swapped(w, "z", N_Z, 2)
        grads, w = lax.optimization_barrier((grads, w))

    def backward(kind, grads, name):
        return call(
            lambda *refs: backward_kernel(kind, *refs),
            name,
            sds((N_Z, XR, F), bf16),
            table,
            tiles,
            grads,
            scratch=[pltpu.VMEM((2 * N_Z + 1, TILE, F), f32)],
        )

    def total(*terms):
        return sum(t.astype(f32) for t in terms).astype(bf16)

    with jax.named_scope("back_crossed"):
        got = xor_swap(backward(3, grads, "back_crossed_far"), "core", 2, 1)
        crossed = total(backward(2, grads, "back_crossed_near"), got)
        crossed, w, grads = lax.optimization_barrier((crossed, w, grads))
    with jax.named_scope("back_own"):
        got = xor_swap(backward(1, grads, "back_own_far"), "core", 2, 1)
        back = total(backward(0, grads, "back_own_near"), got)
    with jax.named_scope("scatter_gradients"):
        away = [across(crossed[a:b]) for a, b in ((0, 1), (1, 3), (3, 5), (5, N_Z))]
        far = total(back[0], away[0][0])
        up, down = shift(far[:HALF], 1), shift(far[HALF:], -1)
        none = jnp.zeros_like(up)
        up, down = jnp.concatenate([up, none], axis=0), jnp.concatenate([none, down], axis=0)
        for d in (3, 2, 1):
            up = shift(total(back[SPOT[d]], away[4 - d][0], up), 1)
            down = shift(total(back[SPOT[N_Z - d]], away[4 - d][1], down), -1)
        grad_features = total(back[SPOT[0]], away[3][2], up, down)
    with jax.named_scope("weight_rest"):
        for axis, n, bit in (("xl", 2, 1), ("z", N_Z, 4), ("xh", 2, 1), ("y", N_Y, 1), ("y", N_Y, 2)):
            w = add_swapped(w, axis, n, bit)
        grad_weight = pl.pallas_call(
            final_weight_kernel,
            out_shape=sds((F, F), f32),
            in_specs=[smem] + [vmem] * 2,
            out_specs=vmem,
            compiler_params=params,
            name="final_weight",
        )(core, w, xor_swap(w, "core", 2, 1))
    return layer_out.reshape(1, 1, XR, F), grad_weight, grad_features


def solution(mesh):
    fine = Mesh(np.asarray(mesh.devices).reshape(N_Y, 2, N_Z, 2, 2), REP + BLK)
    placed = (
        P(REP + BLK, None),
        P(REP, BLK, None, None, None),
        P(REP, BLK, None),
        P(REP, BLK, None),
        P(REP, BLK),
        P(),
        P(BLK, REP, None, None),
    )
    return jax.shard_map(
        on_device,
        mesh=fine,
        in_specs=placed,
        out_specs=(P(BLK, REP, None, None), P(), P(REP + BLK, None)),
        check_vma=False,
    )
```

```python
import jax
import jax.numpy as jnp
import numpy as np
from jax import lax
from jax.experimental import pallas as pl
from jax.experimental.pallas import tpu as pltpu
from jax.sharding import Mesh
from jax.sharding import PartitionSpec as P

REP = ("y", "xh")
BLK = ("z", "xl", "core")
N_Z = 8
N_Y = 4
TILE = 128
F = 256
XR = 256
N_REP = 8
SLOTS = 128
ROW_BLOCKS = 16
UNROLL = 8
HALF = XR // 2
CLASSES = 4
SPOT = {4: 0, 3: 1, 5: 2, 2: 3, 6: 4, 1: 5, 7: 6, 0: 7}

f32 = jnp.float32
bf16 = jnp.bfloat16
VMEM_LIMIT = 16 << 20


def xor_swap(x, axis, n, bit):
    return lax.ppermute(x, axis, [(i, i ^ bit) for i in range(n)])


def add_swapped(x, axis, n, bit):
    return (x.astype(f32) + xor_swap(x, axis, n, bit).astype(f32)).astype(bf16)


def shift(x, step):
    return lax.ppermute(x, "z", [(i, (i + step) % N_Z) for i in range(N_Z)])


def slot_table(rows, cols, count, my_z, my_xl, my_core):
    owner = cols >> 1
    dz = ((owner >> 2) - my_z) & (N_Z - 1)
    dx = ((owner >> 1) & 1) ^ my_xl
    dc = (owner & 1) ^ my_core
    position = jnp.arange(SLOTS, dtype=jnp.int32)
    kind = jnp.where(position < count, 2 * dx + dc, CLASSES)
    spot = jnp.maximum(2 * (4 - jnp.minimum(dz, N_Z - dz)) - 1 + (dz > 4).astype(jnp.int32), 0)
    place = (spot << 1) | (cols & 1)
    packed = rows | (place << 8) | (position << 16)
    key = kind * SLOTS + position
    rank = jnp.sum((key[None, :] < key[:, None]).astype(jnp.int32), axis=1)
    ordered = jnp.sum(jnp.where(rank[None, :] == position[:, None], packed[None, :], 0), axis=1)
    starts = jnp.sum((kind[None, :] < position[:, None]).astype(jnp.int32), axis=1)
    return jnp.concatenate([jnp.stack([ordered, starts]), jnp.zeros((2, SLOTS), jnp.int32)], axis=1)


def slot_range(table, first, last):
    begin = table[1, first]
    return begin, (table[1, last] - begin + UNROLL - 1) // UNROLL


def start_tiles(table, first, last, tiles_hbm, tiles, sems):
    begin, rounds = slot_range(table, first, last)

    def start(i, carry):
        for u in range(UNROLL):
            at = i * UNROLL + u
            pltpu.make_async_copy(tiles_hbm.at[table[0, begin + at] >> 16], tiles.at[at], sems.at[i]).start()
        return carry

    lax.fori_loop(0, rounds, start, 0)


def slot_loop(table, first, last, tiles_hbm, tiles, sems, one_slot):
    begin, rounds = slot_range(table, first, last)
    end = table[1, last]

    def step(i, carry):
        pltpu.make_async_copy(
            tiles_hbm.at[pl.ds(0, UNROLL)], tiles.at[pl.ds(i * UNROLL, UNROLL)], sems.at[i]
        ).wait()
        for u in range(UNROLL):
            t = begin + i * UNROLL + u
            packed = table[0, t]
            one_slot(t < end, packed & 255, (packed >> 8) & 255, tiles[i * UNROLL + u])
        return carry

    lax.fori_loop(0, rounds, step, 0)


def tile_of(ref, which):
    return ref[which >> 1, pl.ds(pl.multiple_of((which & 1) * TILE, TILE), TILE), :]


def blocks(n, one):
    def step(i, carry):
        one(i)
        return carry

    lax.fori_loop(0, n, step, 0)


def clear(acc):
    zero = jnp.zeros((TILE, F), f32)

    def one(i):
        acc[i] = zero

    blocks(acc.shape[0] - 1, one)


def carry_over(before, acc):
    def one(i):
        acc[i] = before[i]

    blocks(acc.shape[0] - 1, one)


def round_out(acc, out):
    def one(i):
        for h in range(2):
            out[i, pl.ds(h * TILE, TILE), :] = acc[2 * i + h].astype(bf16)

    blocks(out.shape[0], one)


def assemble_kernel(*refs):
    out, sems = refs[-2:]
    copies = []
    for k, src in enumerate(refs[:-2]):
        if k < 4:
            dst = out.at[SPOT[k]]
        elif k < 6:
            dst = out.at[SPOT[4], pl.ds((k - 4) * HALF, HALF)]
        else:
            dst = out.at[SPOT[k - 1]]
        copies.append(pltpu.make_async_copy(src, dst, sems.at[k]))
    for c in copies:
        c.start()
    for c in copies:
        c.wait()


def add_products(table, kind, feats, acc, room):
    def one_slot(live, row, place, tile):
        target = jnp.where(live, row, ROW_BLOCKS)
        acc[target] += jnp.dot(tile, tile_of(feats, place), preferred_element_type=f32)

    slot_loop(table, kind, kind + 1, *room, one_slot)


def forward_first_kernel(table, tiles_hbm, near, far, acc, tiles, sems):
    for k in range(2):
        start_tiles(table, k, k + 1, tiles_hbm, tiles.at[k], sems.at[k])
    clear(acc)
    for k, feats in enumerate((near, far)):
        add_products(table, k, feats, acc, (tiles_hbm, tiles.at[k], sems.at[k]))


def forward_near_kernel(table, tiles_hbm, feats, before, acc, tiles, sems):
    start_tiles(table, 2, 3, tiles_hbm, tiles.at[0], sems.at[0])
    carry_over(before, acc)
    add_products(table, 2, feats, acc, (tiles_hbm, tiles.at[0], sems.at[0]))


def forward_far_kernel(table, tiles_hbm, feats, before, out, tiles, sems, acc):
    start_tiles(table, 3, 4, tiles_hbm, tiles.at[0], sems.at[0])
    carry_over(before, acc)
    add_products(table, 3, feats, acc, (tiles_hbm, tiles.at[0], sems.at[0]))
    round_out(acc, out)


def backward_kernel(kind, table, tiles_hbm, grads, out, tiles, sems, acc):
    start_tiles(table, kind, kind + 1, tiles_hbm, tiles.at[0], sems.at[0])
    clear(acc)

    def one_slot(live, row, place, tile):
        target = jnp.where(live, place, 2 * N_Z)
        acc[target] += lax.dot_general(
            tile, tile_of(grads, row), (((0,), (0,)), ((), ())), preferred_element_type=f32
        )

    slot_loop(table, kind, kind + 1, tiles_hbm, tiles.at[0], sems.at[0], one_slot)
    round_out(acc, out)


def half_of(core, which):
    return pl.ds(pl.multiple_of((core[0] if which == 0 else 1 - core[0]) * TILE, TILE), TILE)


def final_weight_kernel(core, mine, other, out):
    out[half_of(core, 0), :] = mine[...].astype(f32)
    out[half_of(core, 1), :] = other[...].astype(f32)


def dense_kernel(core, parts, weight, cot, layer_out, payload, keep, give, terms):
    total = parts[0].astype(f32)
    for r in range(1, N_REP):
        total += parts[r].astype(f32)
    hidden = total.astype(bf16)
    w = weight[...]
    preact = jnp.dot(hidden, w, preferred_element_type=f32)
    gating = jax.nn.sigmoid(preact)
    layer_out[...] = (preact * gating).astype(bf16)
    slope = gating * (1.0 + preact * (1.0 - gating))
    grad_pre = (cot[...].astype(f32) * slope).astype(bf16)
    grad_hidden = lax.dot_general(grad_pre, w, (((1,), (1,)), ((), ())), preferred_element_type=f32).astype(bf16)
    for r in range(N_REP):
        payload[r] = grad_hidden
    terms[...] = lax.dot_general(hidden, grad_pre, (((0,), (0,)), ((), ())), preferred_element_type=f32)
    keep[...] = terms[half_of(core, 0), :].astype(bf16)
    give[...] = terms[half_of(core, 1), :].astype(bf16)


def on_device(node_features, tile_values, tile_row, tile_col, tile_count, weight, cotangent):
    sds = jax.ShapeDtypeStruct
    smem = pl.BlockSpec(memory_space=pltpu.SMEM)
    vmem = pl.BlockSpec(memory_space=pltpu.VMEM)
    params = pltpu.CompilerParams(vmem_limit_bytes=VMEM_LIMIT)
    acc_rows = sds((ROW_BLOCKS + 1, TILE, F), f32)
    hbm = pl.BlockSpec(memory_space=pltpu.HBM)
    tiles = pltpu.with_memory_space_constraint(tile_values[0, 0], pltpu.HBM)

    def tile_room(n):
        return [pltpu.VMEM((n, SLOTS, TILE, TILE), bf16), pltpu.SemaphoreType.DMA((n, SLOTS // UNROLL))]

    my_core = lax.axis_index("core")
    my_xl = lax.axis_index("xl")

    def call(kernel, name, out_shape, *args, scratch=(), rooms=1):
        return pl.pallas_call(
            kernel,
            out_shape=out_shape,
            in_specs=[smem, hbm] + [vmem] * (len(args) - 2),
            out_specs=vmem,
            scratch_shapes=tile_room(rooms) + list(scratch),
            compiler_params=params,
            cost_estimate=pl.CostEstimate(flops=1, transcendentals=0, bytes_accessed=1),
            name=name,
        )(*args)

    def across(x):
        return xor_swap(x, "xl", 2, 1)

    def assemble(chunks, name):
        return pl.pallas_call(
            assemble_kernel,
            out_shape=sds((N_Z, XR, F), bf16),
            in_specs=[pl.BlockSpec(memory_space=pl.ANY)] * len(chunks),
            out_specs=vmem,
            scratch_shapes=[pltpu.SemaphoreType.DMA((len(chunks),))],
            compiler_params=params,
            name=name,
        )(*chunks)

    with jax.named_scope("gather_features"):
        own = node_features
        up1, down1 = shift(own, 1), shift(own, -1)
        own_x = across(own)
        up2, down2 = shift(up1, 1), shift(down1, -1)
        up1_x, down1_x = across(up1), across(down1)
        up2, own_x = lax.optimization_barrier((up2, own_x))
        up3, down3 = shift(up2, 1), shift(down2, -1)
        up2_x, down2_x = across(up2), across(down2)
        up3, up1_x, down1_x = lax.optimization_barrier((up3, up1_x, down1_x))
        low, high = shift(up3[:HALF], 1), shift(down3[HALF:], -1)
        near0 = assemble((pltpu.with_memory_space_constraint(own, pltpu.HBM), down1, down2, down3, low, high, up3, up2, up1), "assemble_own")
        far0 = xor_swap(near0, "core", 2, 1)
        crossed = (own_x, down1_x, down2_x, across(down3), across(low), across(high), across(up3), up2_x, up1_x)
        near1 = assemble(crossed, "assemble_crossed")
        far1 = xor_swap(near1, "core", 2, 1)
    with jax.named_scope("slot_table"):
        table = slot_table(
            tile_row[0, 0], tile_col[0, 0], tile_count[0, 0], lax.axis_index("z"), my_xl, my_core
        )
    with jax.named_scope("tile_products"):
        acc = call(forward_first_kernel, "tile_products_first", acc_rows, table, tiles, near0, far0, rooms=2)
        acc = call(forward_near_kernel, "tile_products_near", acc_rows, table, tiles, near1, acc)
        partial = call(
            forward_far_kernel,
            "tile_products_far",
            sds((N_REP, XR, F), bf16),
            table,
            tiles,
            far1,
            acc,
            scratch=[pltpu.VMEM((ROW_BLOCKS + 1, TILE, F), f32)],
        )
    with jax.named_scope("sum_partials"):
        parts = lax.all_to_all(partial, REP, 0, 0, tiled=True)
    with jax.named_scope("dense"):
        core = my_core.astype(jnp.int32).reshape(1)
        layer_out, payload, keep, give = pl.pallas_call(
            dense_kernel,
            out_shape=(
                sds((XR, F), bf16),
                sds((N_REP, XR, F), bf16),
                sds((TILE, F), bf16),
                sds((TILE, F), bf16),
            ),
            in_specs=[smem] + [vmem] * 3,
            out_specs=[vmem] * 4,
            scratch_shapes=[pltpu.VMEM((F, F), f32)],
            compiler_params=params,
            name="dense",
        )(core, parts, weight, cotangent[0, 0])
    with jax.named_scope("share_gradients"):
        grads = lax.all_to_all(payload, REP, 0, 0, tiled=True)
    with jax.named_scope("weight_z"):
        ring = [(2 * z + c, 2 * (z ^ 1) + (c ^ 1)) for z in range(N_Z) for c in range(2)]
        near_give = xor_swap(give, "core", 2, 1).astype(f32)
        far_give = lax.ppermute(give, ("z", "core"), ring).astype(f32)
        far_keep = xor_swap(keep, "z", N_Z, 1).astype(f32)
        w = ((keep.astype(f32) + near_give) + (far_keep + far_give)).astype(bf16)
        w = add_swapped(w, "z", N_Z, 2)
        grads, w = lax.optimization_barrier((grads, w))

    def backward(kind, grads, name):
        return call(
            lambda *refs: backward_kernel(kind, *refs),
            name,
            sds((N_Z, XR, F), bf16),
            table,
            tiles,
            grads,
            scratch=[pltpu.VMEM((2 * N_Z + 1, TILE, F), f32)],
        )

    def total(*terms):
        return sum(t.astype(f32) for t in terms).astype(bf16)

    with jax.named_scope("back_crossed"):
        got = xor_swap(backward(3, grads, "back_crossed_far"), "core", 2, 1)
        crossed = total(backward(2, grads, "back_crossed_near"), got)
        crossed, w, grads = lax.optimization_barrier((crossed, w, grads))
    with jax.named_scope("back_own"):
        got = xor_swap(backward(1, grads, "back_own_far"), "core", 2, 1)
        back = total(backward(0, grads, "back_own_near"), got)
    with jax.named_scope("scatter_gradients"):
        away = [across(crossed[a:b]) for a, b in ((0, 1), (1, 3), (3, 5), (5, N_Z))]
        far = total(back[0], away[0][0])
        up, down = shift(far[:HALF], 1), shift(far[HALF:], -1)
        none = jnp.zeros_like(up)
        up, down = jnp.concatenate([up, none], axis=0), jnp.concatenate([none, down], axis=0)
        for d in (3, 2, 1):
            up = shift(total(back[SPOT[d]], away[4 - d][0], up), 1)
            down = shift(total(back[SPOT[N_Z - d]], away[4 - d][1], down), -1)
        grad_features = total(back[SPOT[0]], away[3][2], up, down)
    with jax.named_scope("weight_rest"):
        for axis, n, bit in (("xl", 2, 1), ("z", N_Z, 4), ("y", N_Y, 1), ("y", N_Y, 2), ("xh", 2, 1)):
            w = add_swapped(w, axis, n, bit)
        grad_weight = pl.pallas_call(
            final_weight_kernel,
            out_shape=sds((F, F), f32),
            in_specs=[smem] + [vmem] * 2,
            out_specs=vmem,
            compiler_params=params,
            name="final_weight",
        )(core, w, xor_swap(w, "core", 2, 1))
    return layer_out.reshape(1, 1, XR, F), grad_weight, grad_features


def solution(mesh):
    fine = Mesh(np.asarray(mesh.devices).reshape(N_Y, 2, N_Z, 2, 2), REP + BLK)
    placed = (
        P(REP + BLK, None),
        P(REP, BLK, None, None, None),
        P(REP, BLK, None),
        P(REP, BLK, None),
        P(REP, BLK),
        P(),
        P(BLK, REP, None, None),
    )
    return jax.shard_map(
        on_device,
        mesh=fine,
        in_specs=placed,
        out_specs=(P(BLK, REP, None, None), P(), P(REP + BLK, None)),
        check_vma=False,
    )
```
